512 devices in a mesh: seq: 64 (over z, x), tp: 8 (over y, core).
Axes of the slice: x: 4, y: 4, z: 16, core: 2. Of those that a mesh axis runs over, the one named last changes fastest.
Arguments:
- queries: bfloat16 [16384, 4096], P(('seq', 'tp')), may hold values from -6 to 6
- key_states: bfloat16 [16384, 2048], P(('seq', 'tp')), may hold values from -6 to 6
- value_state_rows: bfloat16 [16384, 2048], P(('seq', 'tp')), may hold values from -6 to 6
- out_grad: bfloat16 [16384, 4096], P(('seq', 'tp')), may hold values from -6 to 6
- doc_lengths: int32 [16], replicated, may hold values from 1 to 2048, 16384 in all
Outputs:
- query_grad: bfloat16 [16384, 4096], P(('seq', 'tp'))
- key_gradient: bfloat16 [16384, 2048], P(('seq', 'tp'))
- value_gradient: bfloat16 [16384, 2048], P(('seq', 'tp'))
The draws below stay inside these ranges and needn't reach their ends.
Inputs may be any that keep to these rules, and one draw needn't show every extreme that they name: `doc_lengths`: the documents lie one after another from position 0 and fill all 16384 positions; the longest has exactly 2048 tokens.
All inputs are finite; a program needn't handle non-finite values.
Results may differ from the reference program's by a relative error of at most 0.013.
Values may be sent and summed in bfloat16 or wider, within the bound.
A program may use at most 64 MiB of HBM per device.

```python
import math
import jax
import jax.numpy as jnp
import numpy as np
from jax import lax

QUERY_HEADS = 32
KEY_HEADS = 16
HEAD_SIZE = 128
WINDOW = 1024
TOK_DEV = 256
PACKED_TOKENS = 16384
DOCS = 16
MOST_DOC = 2048


def draw_queries(key, part):
    random_seed_key = jax.random.fold_in(key, 1)
    value_results = jnp.clip(jax.random.normal(random_seed_key, (PACKED_TOKENS, QUERY_HEADS * HEAD_SIZE)), -5.0, 5.0)
    return value_results.astype(jnp.float32).astype(jnp.bfloat16)


def draw_key_states(key, part):
    random_seed_key = jax.random.fold_in(key, 3)
    value_results = jnp.clip(jax.random.normal(random_seed_key, (PACKED_TOKENS, KEY_HEADS * HEAD_SIZE)), -5.0, 5.0)
    return value_results.astype(jnp.float32).astype(jnp.bfloat16)


def steps_of(stream_key, dims, split, least, largest):
    level = 1.0
    for axis_at, blocks in split:
        draws = jax.random.uniform(jax.random.fold_in(jax.random.fold_in(stream_key, 6), axis_at), (blocks,), jnp.float32, least / len(split), largest / len(split))
        level = level * jnp.repeat(jnp.exp(draws), dims[axis_at] // blocks).reshape((-1,) + (1,) * (len(dims) - 1 - axis_at))
    return level


def split_up(amount, total, bound, skew):
    loads = [(1 << 20) // math.isqrt(grade ** skew) + 1 for grade in range(2, amount + 1)]
    spare, holding = total - bound - (amount - 1), [1] * (amount - 1)
    while spare > 0:
        free = [i for i in range(amount - 1) if holding[i] < bound]
        pool, remaining = sum([loads[i] for i in free]), spare
        for i in free:
            extra = min(bound - holding[i], max(1, remaining * loads[i] // pool), spare)
            holding[i] = holding[i] + extra
            spare = spare - extra
    return np.array([bound] + holding)


def uneven_parts(own_key, amount, total, bound, lean):
    if amount == 2:
        one = jax.random.randint(own_key, (), max(1, total - bound), min(bound, total - 1) + 1)
        return jnp.stack([one, total - one])
    lengths = jnp.asarray(split_up(amount, total, bound, lean), jnp.int32)
    pairs = (amount - 1) // 2
    giver, receiver = lengths[1:1 + 2 * pairs:2], lengths[2:2 + 2 * pairs:2]
    slack = jnp.minimum(giver - 1, bound - receiver)
    passed = jax.random.randint(jax.random.fold_in(own_key, 1), (pairs,), 0, 1 << 20) % (slack + 1)
    lengths = lengths.at[1:1 + 2 * pairs:2].set(giver - passed).at[2:2 + 2 * pairs:2].set(receiver + passed)
    return lengths[jax.random.permutation(jax.random.fold_in(own_key, 2), amount)]


def scatter_about(rng, extent, width, reach, pieces=(), kind=jnp.bfloat16):
    gain = steps_of(rng, extent, pieces, -0.22, 0.18) if pieces else 1.0
    drawn = jax.random.normal(rng, extent, jnp.float32) * width * gain
    return jnp.minimum(jnp.maximum(drawn, -reach), reach).astype(kind)


def setup_inputs(seed: int = 0) -> dict:
    keys = jax.random.split(jax.random.key(seed), 6)
    queries = draw_queries(jax.random.fold_in(keys[5], 71), 0)
    key_states = draw_key_states(jax.random.fold_in(keys[5], 71), 0)
    value_state_rows = scatter_about(keys[2], (PACKED_TOKENS, KEY_HEADS * HEAD_SIZE), 1.0, 6.0, ((0, 512),))
    out_grad = scatter_about(keys[3], (PACKED_TOKENS, QUERY_HEADS * HEAD_SIZE), 1.0, 6.0, ((0, 512),))
    doc_lengths = uneven_parts(keys[4], DOCS, PACKED_TOKENS, MOST_DOC, 2).astype(jnp.int32)
    return dict(queries=queries, key_states=key_states, value_state_rows=value_state_rows, out_grad=out_grad, doc_lengths=doc_lengths)


attn_scale = 168.0 ** -0.5
masked_floor = -1.0e30


def doc_index(starts_arr, positions):
    counted = jnp.sum((starts_arr[None, :] <= positions[:, None]).astype(jnp.int32), axis=1)
    return counted.astype(jnp.int32) - 1


def reference(queries, key_states, value_state_rows, out_grad, doc_lengths):
    group_width = QUERY_HEADS // KEY_HEADS
    key_span = TOK_DEV + WINDOW
    block_count = PACKED_TOKENS // TOK_DEV
    starts_arr = (jnp.cumsum(doc_lengths) - doc_lengths).astype(jnp.int32)

    def head_slices(kv_head):
        zero_pad = jnp.zeros((WINDOW, HEAD_SIZE), jnp.bfloat16)
        key_cols = lax.dynamic_slice_in_dim(key_states, kv_head * HEAD_SIZE, HEAD_SIZE, 1)
        value_cols = lax.dynamic_slice_in_dim(value_state_rows, kv_head * HEAD_SIZE, HEAD_SIZE, 1)
        key_padded = jnp.concatenate([zero_pad, key_cols], axis=0)
        value_padded = jnp.concatenate([zero_pad, value_cols], axis=0)
        query_cols = lax.dynamic_slice_in_dim(queries, kv_head * group_width * HEAD_SIZE, group_width * HEAD_SIZE, 1)
        grad_cols = lax.dynamic_slice_in_dim(out_grad, kv_head * group_width * HEAD_SIZE, group_width * HEAD_SIZE, 1)

        def step(carried, block_index):
            key_grad_pad, value_grad_pad = carried
            query_start = (block_index * TOK_DEV).astype(jnp.int32)
            key_tile = lax.dynamic_slice_in_dim(key_padded, query_start, key_span, 0)
            value_tile = lax.dynamic_slice_in_dim(value_padded, query_start, key_span, 0)
            query_rows = lax.dynamic_slice_in_dim(query_cols, query_start, TOK_DEV, 0)
            grad_rows = lax.dynamic_slice_in_dim(grad_cols, query_start, TOK_DEV, 0)
            query_pos = query_start + jnp.arange(TOK_DEV, dtype=jnp.int32)
            key_pos = query_start - WINDOW + jnp.arange(key_span, dtype=jnp.int32)
            allowed = (key_pos[None, :] <= query_pos[:, None]) & (query_pos[:, None] - key_pos[None, :] < WINDOW)
            allowed = allowed & (key_pos[None, :] >= 0)
            allowed = allowed & (doc_index(starts_arr, key_pos)[None, :] == doc_index(starts_arr, query_pos)[:, None])
            key_acc = jnp.zeros((key_span, HEAD_SIZE), jnp.float32)
            value_acc = jnp.zeros((key_span, HEAD_SIZE), jnp.float32)
            query_parts = []
            for member in range(group_width):
                query_block = query_rows[:, member * HEAD_SIZE:(member + 1) * HEAD_SIZE]
                grad_block = grad_rows[:, member * HEAD_SIZE:(member + 1) * HEAD_SIZE]
                raw_scores = jnp.dot(query_block, key_tile.T, preferred_element_type=jnp.float32) * attn_scale
                row_max = jnp.max(jnp.where(allowed, raw_scores, masked_floor), axis=1)
                row_sum = jnp.sum(jnp.where(allowed, jnp.exp(raw_scores - row_max[:, None]), 0.0), axis=1)
                log_total = row_max + jnp.log(row_sum)
                probs = jnp.where(allowed, jnp.exp(raw_scores - log_total[:, None]), 0.0)
                probs_bf = probs.astype(jnp.bfloat16)
                attn_out = jnp.dot(probs_bf, value_tile, preferred_element_type=jnp.float32)
                delta_rows = jnp.sum(grad_block.astype(jnp.float32) * attn_out, axis=1)
                prob_grad = jnp.dot(grad_block, value_tile.T, preferred_element_type=jnp.float32)
                grad_scores = (probs * (prob_grad - delta_rows[:, None]) * attn_scale).astype(jnp.bfloat16)
                query_parts.append(jnp.dot(grad_scores, key_tile, preferred_element_type=jnp.float32).astype(jnp.bfloat16))
                key_acc = key_acc + jnp.dot(grad_scores.T, query_block, preferred_element_type=jnp.float32)
                value_acc = value_acc + jnp.dot(probs_bf.T, grad_block, preferred_element_type=jnp.float32)
            key_grad_pad = lax.dynamic_update_slice_in_dim(
                key_grad_pad, lax.dynamic_slice_in_dim(key_grad_pad, query_start, key_span, 0) + key_acc, query_start, 0)
            value_grad_pad = lax.dynamic_update_slice_in_dim(
                value_grad_pad, lax.dynamic_slice_in_dim(value_grad_pad, query_start, key_span, 0) + value_acc, query_start, 0)
            return (key_grad_pad, value_grad_pad), jnp.concatenate(query_parts, axis=1)

        start_pad = jnp.zeros((PACKED_TOKENS + WINDOW, HEAD_SIZE), jnp.float32)
        (key_grad_pad, value_grad_pad), query_blocks = lax.scan(
            step, (start_pad, start_pad), jnp.arange(block_count, dtype=jnp.int32))
        query_part = query_blocks.reshape(PACKED_TOKENS, group_width * HEAD_SIZE)
        return query_part, key_grad_pad[WINDOW:].astype(jnp.bfloat16), value_grad_pad[WINDOW:].astype(jnp.bfloat16)

    query_matrix, key_matrix, value_matrix = lax.map(head_slices, jnp.arange(KEY_HEADS, dtype=jnp.int32))
    query_grad = jnp.transpose(query_matrix, (1, 0, 2)).reshape(PACKED_TOKENS, QUERY_HEADS * HEAD_SIZE)
    key_gradient = jnp.transpose(key_matrix, (1, 0, 2)).reshape(PACKED_TOKENS, KEY_HEADS * HEAD_SIZE)
    value_gradient = jnp.transpose(value_matrix, (1, 0, 2)).reshape(PACKED_TOKENS, KEY_HEADS * HEAD_SIZE)
    return (query_grad, key_gradient, value_gradient)
```

```python
import functools
import math

import jax
import jax.numpy as jnp
from jax import lax
from jax.experimental import pallas as pl
from jax.experimental.pallas import tpu as pltpu
from jax.sharding import PartitionSpec as P

MESH = pl.DeviceIdType.MESH
HEAD = 128
ROWS = 32
HALF = 512
BLOCK = 256
SPAN = 3 * HALF
WINDOW = 1024
DOCS = 16
SCALE = 168.0 ** (-0.5)
EXP_SCALE = SCALE / math.log(2.0)
FLOOR = -1e30
BF = jnp.bfloat16
F32 = jnp.float32


def dot_nt(a, b):
    return lax.dot_general(a, b, (((1,), (1,)), ((), ())), preferred_element_type=F32)


def dot_nn(a, b):
    return lax.dot_general(a, b, (((1,), (0,)), ((), ())), preferred_element_type=F32)


def dot_tn(a, b):
    return lax.dot_general(a, b, (((0,), (0,)), ((), ())), preferred_element_type=F32)


def block_probs(hd, b, kv, qg, first, probs, grads):
    at = pl.multiple_of(b * BLOCK, BLOCK)
    q = qg[hd, 0, pl.ds(at, BLOCK), :]
    g = qg[hd, 1, pl.ds(at, BLOCK), :]
    low = first[:, pl.ds(at, BLOCK)] - at
    row = lax.broadcasted_iota(jnp.int32, (BLOCK, BLOCK), 0)
    col = lax.broadcasted_iota(jnp.int32, (BLOCK, BLOCK), 1)
    causal = row <= col

    def rows_of(which, t):
        return kv[which, pl.ds(pl.multiple_of(at + t * BLOCK, BLOCK), BLOCK), :]

    def tiles_of(which, other):
        far = dot_nt(rows_of(which, 0), other)
        near = dot_nt(rows_of(which, 4), other)
        return [jnp.where(causal, near, far)] + [
            dot_nt(rows_of(which, t), other) for t in (1, 2, 3)
        ]

    scores = tiles_of(0, q)
    scores = [
        jnp.where(jnp.where(causal, row + 4 * BLOCK, row) >= low, scores[0], FLOOR)
    ] + [
        jnp.where(row >= low - t * BLOCK, scores[t], FLOOR) for t in (1, 2, 3)
    ]
    peak = functools.reduce(
        jnp.maximum, [jnp.max(s, axis=0, keepdims=True) for s in scores]
    )
    powers = [jnp.exp2((s - peak) * EXP_SCALE) for s in scores]
    total = sum(jnp.sum(e, axis=0, keepdims=True) for e in powers)
    inverse = 1.0 / total
    ps = [e * inverse for e in powers]
    dps = tiles_of(1, g)
    delta = sum(
        jnp.sum(p * d, axis=0, keepdims=True) for p, d in zip(ps, dps)
    )
    dss = [p * (d - delta) for p, d in zip(ps, dps)]
    cols = pl.ds(at, BLOCK)

    def put(ref, values):
        zero = jnp.zeros((BLOCK, BLOCK), F32)
        parts = [jnp.where(causal, zero, values[0])] + values[1:]
        parts = parts + [jnp.where(causal, values[0], zero)]
        for t, part in enumerate(parts):
            rows = pl.ds(pl.multiple_of(at + t * BLOCK, BLOCK), BLOCK)
            ref[rows, cols] = part.astype(BF)

    put(probs, ps)
    put(grads, dss)


def seg_grads(hd, seg, qg, probs, grads):
    rows = pl.ds(pl.multiple_of(seg * HALF, HALF), HALF)
    dk = dot_nn(grads[rows, :], qg[hd, 0])
    dv = dot_nn(probs[rows, :], qg[hd, 1])
    return dk, dv


def block_dq(b, kv, grads):
    at = b * BLOCK
    ds = grads[at : at + 5 * BLOCK, at : at + BLOCK]
    return dot_tn(ds, kv[0, at : at + 5 * BLOCK, :])


def kernel(
    compute,
    q_hbm, k_hbm, v_hbm, g_hbm, doc_hbm,
    dq_out, dk_out, dv_out,
    kv, qg, first, probs, grads, acc, dq_st, st1, r1, st0, r0, st2, docs,
    doc_sem, kv_sem, z_sem, o_sem, qg_sem, snd, snd0, snd_z, snd_o,
    x1_s, x1_r, x0_s, x0_r, odq_s, odq_s0, odq_r, okv_s, okv_s0, odk_r, odv_r,
):
    seq = lax.axis_index("seq")
    tp = lax.axis_index("tp")
    z, x = seq // 4, seq % 4
    y, c = tp // 2, tp % 2
    side = x // 2
    slot = (x % 2) * 8 + tp
    head = x * 4 + y
    up = (((z + 1) % 16) * 4 + x, tp)
    down = (((z + 15) % 16) * 4 + x, tp)
    other = (seq, y * 2 + (1 - c))

    doc_copy = pltpu.make_async_copy(doc_hbm, docs, doc_sem)
    doc_copy.start()

    barrier = pltpu.get_barrier_semaphore()

    def greet(i, carry):
        tx, ty, tc = (x + i // 8) % 4, (y + (i // 2) % 4) % 4, (c + i % 2) % 2
        pl.semaphore_signal(
            barrier, inc=1, device_id=(z * 4 + tx, ty * 2 + tc), device_id_type=MESH
        )
        return carry

    lax.fori_loop(1, 32, greet, 0)
    for peer in (up, down):
        pl.semaphore_signal(barrier, inc=1, device_id=peer, device_id_type=MESH)
    pl.semaphore_wait(barrier, 33)

    def key_rows(at):
        return pl.ds(pl.multiple_of(at, ROWS), ROWS)

    def in_pairs(h):
        kcols = pl.ds(pl.multiple_of(h * HEAD, HEAD), HEAD)
        pairs = [
            (k_hbm.at[:, kcols], kv.at[0, key_rows(WINDOW + ROWS * slot), :], kv_sem.at[slot]),
            (v_hbm.at[:, kcols], kv.at[1, key_rows(WINDOW + ROWS * slot), :], kv_sem.at[slot]),
        ]
        for hd in range(2):
            qcols = pl.ds(pl.multiple_of(h * 2 * HEAD + hd * HEAD, HEAD), HEAD)
            for j, ref in enumerate((q_hbm, g_hbm)):
                pairs.append(
                    (ref.at[:, qcols], qg.at[hd, j, key_rows(ROWS * slot), :], qg_sem.at[hd])
                )
        return pairs

    def remote(src, dst, send, recv, dev):
        pltpu.make_async_remote_copy(
            src_ref=src, dst_ref=dst, send_sem=send, recv_sem=recv,
            device_id=dev, device_id_type=MESH,
        ).start()

    def send_in(kinds):
        @pl.when(c == side)
        def _():
            for src, dst, sem in in_pairs(head)[kinds]:
                pltpu.make_async_copy(src, dst, sem).start()

        @pl.when(c != side)
        def _():
            for src, dst, sem in in_pairs(head)[kinds]:
                remote(src, dst, snd0, sem, (seq, y * 2 + side))

        def step(i, carry):
            tx = (x + i % 4) % 4
            ty = (y + i % 4 + i // 4) % 4
            for src, dst, sem in in_pairs(tx * 4 + ty)[kinds]:
                remote(src, dst, snd, sem, (z * 4 + tx, ty * 2 + side))
            return carry

        lax.fori_loop(1, 16, step, 0)

    send_in(slice(0, 2))
    send_in(slice(2, 4))
    send_in(slice(4, 6))

    def bytes_of(ref, sem):
        return pltpu.make_async_copy(ref, ref, sem)

    doc_copy.wait()
    base = z * 1024 + c * HALF - WINDOW
    pos = lax.broadcasted_iota(jnp.int32, (1, HALF), 1) + (base + WINDOW)
    low = jnp.zeros((1, HALF), jnp.int32)
    start = jnp.int32(0)
    for d in range(DOCS):
        low = jnp.where(pos >= start, start, low)
        start = start + docs[d]
    first[...] = low - base

    zero = jnp.zeros((BLOCK, BLOCK), BF)
    for ref in (probs, grads):
        ref[0:BLOCK, BLOCK : 2 * BLOCK] = zero
        ref[SPAN - BLOCK : SPAN, 0:BLOCK] = zero

    def relay(s, carry):
        mine = kv.at[:, key_rows(WINDOW + ROWS * s), :]
        bytes_of(mine, kv_sem.at[s]).wait()
        remote(mine, kv.at[:, key_rows(ROWS * s), :], snd_z, z_sem.at[s], up)

        @pl.when(c == 0)
        def _():
            remote(mine, kv.at[:, key_rows(HALF + ROWS * s), :], snd_o, o_sem, other)

        return carry

    lax.fori_loop(0, 16, relay, 0)

    def relay_core(s, carry):
        mine = kv.at[:, key_rows(ROWS * s), :]
        bytes_of(mine, z_sem.at[s]).wait()

        @pl.when(c == 1)
        def _():
            remote(mine, kv.at[:, key_rows(HALF + ROWS * s), :], snd_o, o_sem, other)

        return carry

    lax.fori_loop(0, 16, relay_core, 0)
    bytes_of(kv.at[:, HALF:WINDOW, :], o_sem).wait()

    def owner(i):
        s = (slot + i) % 16
        return s, (z * 4 + 2 * c + s // 8, s % 8)

    def send_out(i, pairs_of, sem0, sem):
        pass

    def out_dq(hd):
        cols = pl.ds(pl.multiple_of(head * 2 * HEAD + hd * HEAD, HEAD), HEAD)
        dst = dq_out.at[:, cols]

        def src(s):
            return dq_st.at[hd, key_rows(ROWS * s), :]

        @pl.when(c == side)
        def _():
            pltpu.make_async_copy(src(slot), dst, odq_r).start()

        @pl.when(c != side)
        def _():
            s, dev = owner(0)
            remote(src(s), dst, odq_s0, odq_r, dev)

        def step(i, carry):
            s, dev = owner(i)
            remote(src(s), dst, odq_s, odq_r, dev)
            return carry

        lax.fori_loop(1, 16, step, 0)

    def do_dq(hd):
        if compute:
            for b in range(2):
                dq_st[hd, b * BLOCK : (b + 1) * BLOCK, :] = (
                    block_dq(b, kv, grads) * SCALE
                ).astype(BF)
        else:
            dq_st[hd] = qg[hd, 0]
        out_dq(hd)

    def do_probs(hd):
        bytes_of(qg.at[hd], qg_sem.at[hd]).wait()
        if compute:

            def one(b, carry):
                block_probs(hd, b, kv, qg, first, probs, grads)
                return carry

            lax.fori_loop(0, 2, one, 0)

    def grads_of(hd, seg):
        if compute:
            return seg_grads(hd, seg, qg, probs, grads)
        return qg[hd, 0].astype(F32), qg[hd, 1].astype(F32)

    def seg_rows(seg):
        return pl.ds(pl.multiple_of(seg * HALF, HALF), HALF)

    do_probs(0)

    def first_head(seg, carry):
        dk, dv = grads_of(0, seg)
        acc[0, seg_rows(seg), :] = dk
        acc[1, seg_rows(seg), :] = dv
        return carry

    lax.fori_loop(0, 3, first_head, 0)
    do_dq(0)
    do_probs(1)

    def add_up(seg):
        dk, dv = grads_of(1, seg)
        acc[0, seg_rows(seg), :] += dk
        acc[1, seg_rows(seg), :] += dv

    def ship_middle():
        st1[...] = acc[:, HALF:WINDOW, :].astype(BF)
        remote(st1, r1, x1_s, x1_r, other)

    @pl.when(c == 0)
    def _():
        add_up(1)
        ship_middle()
        add_up(0)
        st0[...] = acc[:, 0:HALF, :].astype(BF)

    @pl.when(c == 1)
    def _():
        add_up(0)
        add_up(1)
        ship_middle()

    CH = 4
    CR = HALF // CH

    @pl.when(c == 1)
    def _():
        bytes_of(r1, x1_r).wait()
        st0[...] = (acc[:, 0:HALF, :] + r1[...].astype(F32)).astype(BF)

    for ch in range(CH):
        remote(
            st0.at[:, ch * CR : (ch + 1) * CR, :], r0.at[:, ch * CR : (ch + 1) * CR, :],
            x0_s, x0_r.at[ch], down,
        )
    add_up(2)
    do_dq(1)

    @pl.when(c == 0)
    def _():
        bytes_of(r1, x1_r).wait()
        acc[:, WINDOW:SPAN, :] += r1[...].astype(F32)

    kcols = pl.ds(pl.multiple_of(head * HEAD, HEAD), HEAD)

    def out_pairs(s):
        return (
            (st2.at[0, key_rows(ROWS * s), :], dk_out.at[:, kcols], odk_r),
            (st2.at[1, key_rows(ROWS * s), :], dv_out.at[:, kcols], odv_r),
        )

    def finish(ch, carry):
        rows = pl.ds(pl.multiple_of(ch * CR, CR), CR)
        bytes_of(r0.at[:, rows, :], x0_r.at[ch]).wait()
        late = pl.ds(pl.multiple_of(WINDOW + ch * CR, CR), CR)
        whole = acc[:, late, :] + r0[:, rows, :].astype(F32)
        st2[0, rows, :] = (whole[0] * SCALE).astype(BF)
        st2[1, rows, :] = whole[1].astype(BF)

        def step(j, inner):
            s = ch * 4 + j
            dev = (z * 4 + 2 * c + s // 8, s % 8)
            here = (s == slot) & (c == side)

            @pl.when(here)
            def _():
                for src, dst, sem in out_pairs(s):
                    pltpu.make_async_copy(src, dst, sem).start()

            @pl.when(jnp.logical_not(here))
            def _():
                for src, dst, sem in out_pairs(s):
                    remote(src, dst, okv_s, sem, dev)

            return inner

        return lax.fori_loop(0, 4, step, carry)

    lax.fori_loop(0, CH, finish, 0)

    bytes_of(kv.at[:, 0:1440, :], snd).wait()

    @pl.when(c != side)
    def _():
        bytes_of(kv.at[:, 0:96, :], snd0).wait()
        bytes_of(dq_st.at[:, 0:ROWS, :], odq_s0).wait()
        bytes_of(st2, okv_s).wait()

    @pl.when(c == side)
    def _():
        bytes_of(st2.at[:, 0 : HALF - ROWS, :], okv_s).wait()

    bytes_of(kv.at[:, 0:HALF, :], snd_z).wait()
    bytes_of(kv.at[:, 0:HALF, :], snd_o).wait()
    bytes_of(st1, x1_s).wait()
    bytes_of(st0, x0_s).wait()
    bytes_of(dq_st.at[:, 0 : HALF - ROWS, :], odq_s).wait()
    bytes_of(dq_out, odq_r).wait()
    bytes_of(dk_out, odk_r).wait()
    bytes_of(dv_out, odv_r).wait()


def per_device(compute, queries, key_states, value_state_rows, out_grad, doc_lengths):
    any_space = pl.BlockSpec(memory_space=pl.ANY)
    dma = pltpu.SemaphoreType.DMA
    return pl.pallas_call(
        functools.partial(kernel, compute),
        out_shape=(
            jax.ShapeDtypeStruct(queries.shape, BF),
            jax.ShapeDtypeStruct(key_states.shape, BF),
            jax.ShapeDtypeStruct(value_state_rows.shape, BF),
        ),
        in_specs=[any_space] * 5,
        out_specs=(any_space,) * 3,
        scratch_shapes=[
            pltpu.VMEM((2, SPAN, HEAD), BF),
            pltpu.VMEM((2, 2, HALF, HEAD), BF),
            pltpu.VMEM((1, HALF), jnp.int32),
            pltpu.VMEM((SPAN, HALF), BF),
            pltpu.VMEM((SPAN, HALF), BF),
            pltpu.VMEM((2, SPAN, HEAD), F32),
            pltpu.VMEM((2, HALF, HEAD), BF),
            pltpu.VMEM((2, HALF, HEAD), BF),
            pltpu.VMEM((2, HALF, HEAD), BF),
            pltpu.VMEM((2, HALF, HEAD), BF),
            pltpu.VMEM((2, HALF, HEAD), BF),
            pltpu.VMEM((2, HALF, HEAD), BF),
            pltpu.SMEM((DOCS,), jnp.int32),
            dma, dma((16,)), dma((16,)), dma, dma((2,)), dma, dma, dma, dma,
            dma, dma, dma, dma((4,)), dma, dma, dma, dma, dma, dma, dma,
        ],
        compiler_params=pltpu.CompilerParams(
            collective_id=0, has_side_effects=True, vmem_limit_bytes=60 * 1024 * 1024
        ),
        name="window_attention_backward",
    )(queries, key_states, value_state_rows, out_grad, doc_lengths)


COMPUTE = True


def solution(mesh):
    rows = P(("seq", "tp"), None)
    return jax.shard_map(
        functools.partial(per_device, COMPUTE),
        mesh=mesh,
        in_specs=(rows, rows, rows, rows, P()),
        out_specs=(rows, rows, rows),
        check_vma=False,
    )
```

```python
import functools
import math

import jax
import jax.numpy as jnp
from jax import lax
from jax.experimental import pallas as pl
from jax.experimental.pallas import tpu as pltpu
from jax.sharding import PartitionSpec as P

MESH = pl.DeviceIdType.MESH
HEAD = 128
ROWS = 32
HALF = 512
BLOCK = 256
SPAN = 3 * HALF
WINDOW = 1024
DOCS = 16
PLANES = 16
SCALE = 168.0 ** (-0.5)
EXP_SCALE = SCALE / math.log(2.0)
FLOOR = -1e30
BF = jnp.bfloat16
F32 = jnp.float32


def dot_nt(a, b):
    return lax.dot_general(a, b, (((1,), (1,)), ((), ())), preferred_element_type=F32)


def dot_nn(a, b):
    return lax.dot_general(a, b, (((1,), (0,)), ((), ())), preferred_element_type=F32)


def dot_tn(a, b):
    return lax.dot_general(a, b, (((0,), (0,)), ((), ())), preferred_element_type=F32)


def unit(hd, j, at, kv, qg, first, acc, dq):
    qrows = pl.ds(pl.multiple_of(j * BLOCK, BLOCK), BLOCK)
    q = qg[hd, 0, qrows, :]
    g = qg[hd, 1, qrows, :]
    low = first[:, qrows] - at
    row = lax.broadcasted_iota(jnp.int32, (BLOCK, BLOCK), 0)
    col = lax.broadcasted_iota(jnp.int32, (BLOCK, BLOCK), 1)
    causal = row <= col
    def rows_at(t):
        return pl.ds(pl.multiple_of(at + t * BLOCK, BLOCK), BLOCK)
    def tiles_of(which, w):
        far = dot_nt(kv[which, rows_at(0), :], w)
        near = dot_nt(kv[which, rows_at(4), :], w)
        return [jnp.where(causal, near, far)] + [dot_nt(kv[which, rows_at(t), :], w) for t in (1, 2, 3)]
    scores = tiles_of(0, q)
    scores = [jnp.where(jnp.where(causal, row + 4 * BLOCK, row) >= low, scores[0], FLOOR)] + [
        jnp.where(row >= low - t * BLOCK, scores[t], FLOOR) for t in (1, 2, 3)]
    peak = functools.reduce(jnp.maximum, scores)
    peak = jnp.max(peak, axis=0, keepdims=True) * EXP_SCALE
    ps = [jnp.exp2(s * EXP_SCALE - peak) for s in scores]
    total = jnp.sum(functools.reduce(jnp.add, ps), axis=0, keepdims=True)
    inverse = 1.0 / total
    dps = tiles_of(1, g)
    ps = [p * inverse for p in ps]
    ts = [p * d for p, d in zip(ps, dps)]
    delta = jnp.sum(functools.reduce(jnp.add, ts), axis=0, keepdims=True)
    dss = [t - p * delta for p, t in zip(ps, ts)]
    zero = jnp.zeros((BLOCK, BLOCK), F32)
    def spread(v):
        parts = [jnp.where(causal, zero, v[0])] + v[1:] + [jnp.where(causal, v[0], zero)]
        return [p.astype(BF) for p in parts]
    pb = spread(ps); db = spread(dss)
    for t in range(5):
        acc[1, rows_at(t), :] += dot_nn(pb[t], g)
        acc[0, rows_at(t), :] += dot_nn(db[t], q)
    out = functools.reduce(
        jnp.add, [dot_tn(db[t], kv[0, rows_at(t), :]) for t in range(5)]
    )
    cols = pl.ds(pl.multiple_of(hd * HEAD, HEAD), HEAD)
    dq[qrows, cols] = (out * SCALE).astype(BF)


VLIM = 64800
PUT = True
OUT_SHAPE = pltpu.VMEM


def OUT_SPEC():
    return pl.BlockSpec(memory_space=pltpu.VMEM)


def PUT_SPEC():
    return pl.BlockSpec(memory_space=pltpu.VMEM)


def kernel(
    q_hbm, k_hbm, v_hbm, g_hbm, doc_hbm,
    dq_out, dk_out, dv_out,
    kv, qg, first, acc, dq_st, st1, r1, st0, r0, st2, docs,
    doc_sem, kv_sem, z_sem, o_sem, qg_sem, snd, snd0, snd_z, snd_o, snd_o2,
    x1_s, x1_r, x0_s, x0_r, odq_s, odq_r, okv_s, odk_r, odv_r,
):
    seq = lax.axis_index("seq")
    tp = lax.axis_index("tp")
    z, x = seq // 4, seq % 4
    y, c = tp // 2, tp % 2
    side = x % 2
    slot = (x // 2) * 8 + tp
    head = x * 4 + y
    first_plane, last_plane = z == 0, z == PLANES - 1
    up = (((z + 1) % PLANES) * 4 + x, tp)
    down = (((z + PLANES - 1) % PLANES) * 4 + x, tp)
    other = (seq, y * 2 + (1 - c))

    doc_copy = pltpu.make_async_copy(doc_hbm, docs, doc_sem)
    doc_copy.start()

    barrier = pltpu.get_barrier_semaphore()
    xs = [(x + d) % 4 for d in range(4)]
    ys = [(y + d) % 4 for d in range(4)]
    for dx, dy in sorted(
        ((a, b) for a in range(4) for b in range(4)),
        key=lambda p: -(min(p[0], 4 - p[0]) + min(p[1], 4 - p[1])),
    ):
        for tc in (1 - c, c) if (dx, dy) != (0, 0) else (1 - c,):
            pl.semaphore_signal(
                barrier, inc=1, device_id=(z * 4 + xs[dx], ys[dy] * 2 + tc),
                device_id_type=MESH,
            )

    @pl.when(z < PLANES - 1)
    def _():
        pl.semaphore_signal(barrier, inc=1, device_id=up, device_id_type=MESH)

    @pl.when(z > 0)
    def _():
        pl.semaphore_signal(barrier, inc=1, device_id=down, device_id_type=MESH)

    acc[...] = jnp.zeros(acc.shape, F32)

    @pl.when(first_plane)
    def _():
        kv[:, 0:WINDOW, :] = jnp.zeros((2, WINDOW, HEAD), BF)

    @pl.when(last_plane)
    def _():
        r0[...] = jnp.zeros(r0.shape, BF)

    pl.semaphore_wait(barrier, 33 - z // (PLANES - 1) - (PLANES - 1 - z) // (PLANES - 1))

    def key_rows(at):
        return pl.ds(pl.multiple_of(at, ROWS), ROWS)

    def remote(src, dst, send, recv, dev):
        pltpu.make_async_remote_copy(
            src_ref=src, dst_ref=dst, send_sem=send, recv_sem=recv,
            device_id=dev, device_id_type=MESH,
        ).start()

    def bytes_of(ref, sem):
        return pltpu.make_async_copy(ref, ref, sem)

    my_keys = key_rows(WINDOW + x * BLOCK + ROWS * tp)
    my_rows = key_rows(ROWS * slot)

    def in_pairs(h):
        kcols = pl.ds(pl.multiple_of(h * HEAD, HEAD), HEAD)
        pairs = [
            (k_hbm.at[:, kcols], kv.at[0, my_keys, :], kv_sem.at[slot]),
            (v_hbm.at[:, kcols], kv.at[1, my_keys, :], kv_sem.at[slot]),
        ]
        for hd in range(2):
            qcols = pl.ds(pl.multiple_of(h * 2 * HEAD + hd * HEAD, HEAD), HEAD)
            for j, ref in enumerate((q_hbm, g_hbm)):
                pairs.append((ref.at[:, qcols], qg.at[hd, j, my_rows, :], qg_sem.at[hd]))
        return pairs

    def send_here(kinds):
        @pl.when(c == side)
        def _():
            for src, dst, sem in in_pairs(head)[kinds]:
                pltpu.make_async_copy(src, dst, sem).start()

        @pl.when(c != side)
        def _():
            for src, dst, sem in in_pairs(head)[kinds]:
                remote(src, dst, snd0, sem, other)

    def send_away(kinds, i):
        tx = (x + i % 4) % 4
        ty = (y + i % 4 + i // 4) % 4
        for src, dst, sem in in_pairs(tx * 4 + ty)[kinds]:
            remote(src, dst, snd, sem, (z * 4 + tx, ty * 2 + side))

    KEYS, HEAD0, HEAD1 = slice(0, 2), slice(2, 4), slice(4, 6)

    def send_all(kinds):
        def step(i, carry):
            send_away(kinds, i)
            return carry

        lax.fori_loop(1, 16, step, 0)

    send_all(KEYS)
    send_here(KEYS)
    send_all(HEAD0)
    send_here(HEAD0)
    send_here(HEAD1)

    doc_copy.wait()
    for j in range(2):
        begin = z * 1024 + (2 * j + c) * BLOCK
        pos = lax.broadcasted_iota(jnp.int32, (1, BLOCK), 1) + begin
        low = jnp.zeros((1, BLOCK), jnp.int32)
        start = jnp.int32(0)
        for d in range(DOCS):
            low = jnp.where(pos >= start, start, low)
            start = start + docs[d]
        first[:, j * BLOCK : (j + 1) * BLOCK] = low - (z - 1) * 1024

    def relay(s):
        mine = kv.at[:, key_rows(WINDOW + (2 * (s // 8) + c) * BLOCK + ROWS * (s % 8)), :]
        ahead = kv.at[:, key_rows((2 * (s // 8) + c) * BLOCK + ROWS * (s % 8)), :]
        bytes_of(mine, kv_sem.at[s]).wait()

        @pl.when(z < PLANES - 1)
        def _():
            remote(mine, ahead, snd_z, z_sem.at[s], up)

        remote(mine, mine, snd_o, o_sem, other)

    relay(0)

    def relay_send(s, carry):
        relay(s)
        send_away(HEAD1, s)
        return carry

    lax.fori_loop(1, 16, relay_send, 0)

    def relay_core(s, carry):
        mine = kv.at[:, key_rows((2 * (s // 8) + c) * BLOCK + ROWS * (s % 8)), :]
        bytes_of(mine, z_sem.at[s]).wait()
        remote(mine, mine, snd_o2, o_sem, other)
        return carry

    @pl.when(z > 0)
    def _():
        lax.fori_loop(0, 16, relay_core, 0)
        bytes_of(kv.at[:, 0:WINDOW, :], o_sem).wait()

    @pl.when(first_plane)
    def _():
        bytes_of(kv.at[:, 0:HALF, :], o_sem).wait()

    def run_unit(hd, j):
        at = pl.multiple_of((2 * j + c) * BLOCK, BLOCK)
        if COMPUTE:
            unit(hd, j, at, kv, qg, first, acc, dq_st)

    def first_head(j, carry):
        run_unit(0, j)
        return carry

    def tile(t):
        return acc[:, pl.ds(pl.multiple_of(t * BLOCK, BLOCK), BLOCK), :]

    def ship_core(m, t):
        st1[m] = tile(t).astype(BF)
        remote(st1.at[m], r1.at[m], x1_s, x1_r.at[m], other)

    def ship_down(i, total):
        st0[i] = total.astype(BF)

        @pl.when(z > 0)
        def _():
            for h in range(2):
                part = slice(h * 128, (h + 1) * 128)
                remote(
                    st0.at[i, :, part, :], r0.at[i, :, part, :],
                    x0_s, x0_r.at[2 * i + h], down,
                )

    bytes_of(qg.at[0], qg_sem.at[0]).wait()
    lax.fori_loop(0, 2, first_head, 0)
    bytes_of(qg.at[1], qg_sem.at[1]).wait()
    run_unit(1, 0)

    ship_core(0, 1 + c)

    @pl.when(c == 0)
    def _():
        ship_down(0, tile(0))

    @pl.when(c == 1)
    def _():
        bytes_of(r1.at[0], x1_r.at[0]).wait()
        ship_down(0, tile(1) + r1[0].astype(F32))

    run_unit(1, 1)

    ship_core(1, 3 + c)

    @pl.when(c == 0)
    def _():
        bytes_of(r1.at[0], x1_r.at[0]).wait()
        ship_down(1, tile(2) + r1[0].astype(F32))

    ship_core(2, 5 + c)
    bytes_of(r1.at[1], x1_r.at[1]).wait()

    @pl.when(c == 1)
    def _():
        ship_down(1, tile(3) + r1[1].astype(F32))

    own = c == side

    def send_out(s, pairs, sem0):
        dev = (z * 4 + 2 * (s // 8) + c, s % 8)
        here = own & (s == slot)

        @pl.when(here)
        def _():
            for src, dst, sem in pairs:
                pltpu.make_async_copy(src, dst, sem).start()

        @pl.when(jnp.logical_not(here))
        def _():
            for src, dst, sem in pairs:
                remote(src, dst, sem0, sem, dev)

    qcols = pl.ds(pl.multiple_of(head * 2 * HEAD, 2 * HEAD), 2 * HEAD)
    kcols = pl.ds(pl.multiple_of(head * HEAD, HEAD), HEAD)

    def dq_step(i, carry):
        s = (slot + i) % 16
        send_out(s, [(dq_st.at[key_rows(ROWS * s), :], dq_out.at[:, qcols], odq_r)], odq_s)
        return carry

    lax.fori_loop(0, 16, dq_step, 0)

    def finish(j, rows, extra):
        at = pl.ds(pl.multiple_of(WINDOW + (2 * j + c) * BLOCK + rows.start, 128), rows.stop - rows.start)
        whole = acc[:, at, :] + r0[j, :, rows, :].astype(F32)
        if extra is not None:
            whole = whole + extra[:, rows, :].astype(F32)
        here = slice(j * BLOCK + rows.start, j * BLOCK + rows.stop)
        st2[0, here, :] = (whole[0] * SCALE).astype(BF)
        st2[1, here, :] = whole[1].astype(BF)

        def step(i, carry):
            s = j * 8 + rows.start // ROWS + i
            send_out(
                s,
                [
                    (st2.at[0, key_rows(ROWS * s), :], dk_out.at[:, kcols], odk_r),
                    (st2.at[1, key_rows(ROWS * s), :], dv_out.at[:, kcols], odv_r),
                ],
                okv_s,
            )
            return carry

        lax.fori_loop(0, (rows.stop - rows.start) // ROWS, step, 0)

    bytes_of(r1.at[2], x1_r.at[2]).wait()
    def await_down(i, h):
        @pl.when(z < PLANES - 1)
        def _():
            bytes_of(r0.at[i, :, h * 128 : (h + 1) * 128, :], x0_r.at[2 * i + h]).wait()

    await_down(0, 0)
    await_down(0, 1)
    finish(0, slice(0, BLOCK), r1.at[1 + c])

    @pl.when(c == 0)
    def _():
        acc[:, WINDOW + 2 * BLOCK : WINDOW + 3 * BLOCK, :] += r1[2].astype(F32)

    for h in range(2):
        rows = slice(h * 128, (h + 1) * 128)
        await_down(1, h)
        finish(1, rows, None)

    bytes_of(kv.at[:, 0:1440, :], snd).wait()

    @pl.when(jnp.logical_not(own))
    def _():
        bytes_of(kv.at[:, 0:96, :], snd0).wait()
        bytes_of(dq_st, odq_s).wait()
        bytes_of(st2, okv_s).wait()

    @pl.when(own)
    def _():
        bytes_of(dq_st.at[0 : HALF - ROWS, :], odq_s).wait()
        bytes_of(st2.at[:, 0 : HALF - ROWS, :], okv_s).wait()

    bytes_of(kv.at[:, 0:HALF, :], snd_o).wait()
    bytes_of(st1, x1_s).wait()

    @pl.when(z < PLANES - 1)
    def _():
        bytes_of(kv.at[:, 0:HALF, :], snd_z).wait()

    @pl.when(z > 0)
    def _():
        bytes_of(kv.at[:, 0:HALF, :], snd_o2).wait()
        bytes_of(st0, x0_s).wait()
    bytes_of(dq_out, odq_r).wait()
    bytes_of(dk_out, odk_r).wait()
    bytes_of(dv_out, odv_r).wait()


def put_kernel(a, b, d, oa, ob, od, sem):
    copies = [
        pltpu.make_async_copy(src, dst, sem.at[i])
        for i, (src, dst) in enumerate(((a, oa), (b, ob), (d, od)))
    ]
    for copy in copies:
        copy.start()
    for copy in copies:
        copy.wait()


def per_device(queries, key_states, value_state_rows, out_grad, doc_lengths):
    any_space = pl.BlockSpec(memory_space=pl.ANY)
    vmem_space = pl.BlockSpec(memory_space=pltpu.VMEM)
    dma = pltpu.SemaphoreType.DMA
    shapes = [queries.shape, key_states.shape, value_state_rows.shape]
    results = pl.pallas_call(
        kernel,
        out_shape=tuple(OUT_SHAPE(s, BF) for s in shapes),
        in_specs=[pl.BlockSpec(memory_space=pltpu.HBM)] * 5,
        out_specs=(OUT_SPEC(),) * 3,
        scratch_shapes=[
            pltpu.VMEM((2, 2 * WINDOW, HEAD), BF),
            pltpu.VMEM((2, 2, HALF, HEAD), BF),
            pltpu.VMEM((1, HALF), jnp.int32),
            pltpu.VMEM((2, 2 * WINDOW, HEAD), F32),
            pltpu.VMEM((HALF, 2 * HEAD), BF),
            pltpu.VMEM((3, 2, BLOCK, HEAD), BF),
            pltpu.VMEM((3, 2, BLOCK, HEAD), BF),
            pltpu.VMEM((2, 2, BLOCK, HEAD), BF),
            pltpu.VMEM((2, 2, BLOCK, HEAD), BF),
            pltpu.VMEM((2, HALF, HEAD), BF),
            pltpu.SMEM((DOCS,), jnp.int32),
            dma, dma((16,)), dma((16,)), dma, dma((2,)), dma, dma, dma, dma, dma,
            dma, dma((3,)), dma, dma((4,)), dma, dma, dma, dma, dma,
        ],
        compiler_params=pltpu.CompilerParams(
            collective_id=0, has_side_effects=True, vmem_limit_bytes=VLIM * 1024
        ),
        name="window_attention_backward",
    )(queries, key_states, value_state_rows, out_grad, doc_lengths)
    if not PUT:
        return results
    return pl.pallas_call(
        put_kernel,
        out_shape=tuple(jax.ShapeDtypeStruct(s, BF) for s in shapes),
        in_specs=[PUT_SPEC()] * 3,
        out_specs=(any_space,) * 3,
        scratch_shapes=[dma((3,))],
        compiler_params=pltpu.CompilerParams(vmem_limit_bytes=1024 * 1024),
        name="put_results",
    )(*results)


COMPUTE = True


def solution(mesh):
    rows = P(("seq", "tp"), None)
    return jax.shard_map(
        per_device,
        mesh=mesh,
        in_specs=(rows, rows, rows, rows, P()),
        out_specs=(rows, rows, rows),
        check_vma=False,
    )
```

```python
import functools
import math

import jax
import jax.numpy as jnp
from jax import lax
from jax.experimental import pallas as pl
from jax.experimental.pallas import tpu as pltpu
from jax.sharding import PartitionSpec as P

MESH = pl.DeviceIdType.MESH
HEAD = 128
ROWS = 32
HALF = 512
BLOCK = 256
SPAN = 3 * HALF
WINDOW = 1024
DOCS = 16
PLANES = 16
SCALE = 168.0 ** (-0.5)
EXP_SCALE = SCALE / math.log(2.0)
FLOOR = -1e30
BF = jnp.bfloat16
F32 = jnp.float32


def dot_nt(a, b):
    return lax.dot_general(a, b, (((1,), (1,)), ((), ())), preferred_element_type=F32)


def dot_nn(a, b):
    return lax.dot_general(a, b, (((1,), (0,)), ((), ())), preferred_element_type=F32)


def dot_tn(a, b):
    return lax.dot_general(a, b, (((0,), (0,)), ((), ())), preferred_element_type=F32)


def unit(hd, j, at, kv, qg, first, acc, dq):
    qrows = pl.ds(pl.multiple_of(j * BLOCK, BLOCK), BLOCK)
    q = qg[hd, 0, qrows, :]
    g = qg[hd, 1, qrows, :]
    low = first[:, qrows] - at
    row = lax.broadcasted_iota(jnp.int32, (BLOCK, BLOCK), 0)
    col = lax.broadcasted_iota(jnp.int32, (BLOCK, BLOCK), 1)
    causal = row <= col
    def rows_at(t):
        return pl.ds(pl.multiple_of(at + t * BLOCK, BLOCK), BLOCK)
    def tiles_of(which, w):
        far = dot_nt(kv[which, rows_at(0), :], w)
        near = dot_nt(kv[which, rows_at(4), :], w)
        return [jnp.where(causal, near, far)] + [dot_nt(kv[which, rows_at(t), :], w) for t in (1, 2, 3)]
    scores = tiles_of(0, q)
    scores = [jnp.where(jnp.where(causal, row + 4 * BLOCK, row) >= low, scores[0], FLOOR)] + [
        jnp.where(row >= low - t * BLOCK, scores[t], FLOOR) for t in (1, 2, 3)]
    peak = functools.reduce(jnp.maximum, scores)
    peak = jnp.max(peak, axis=0, keepdims=True) * EXP_SCALE
    ps = [jnp.exp2(s * EXP_SCALE - peak) for s in scores]
    total = jnp.sum(functools.reduce(jnp.add, ps), axis=0, keepdims=True)
    inverse = 1.0 / total
    dps = tiles_of(1, g)
    ps = [p * inverse for p in ps]
    ts = [p * d for p, d in zip(ps, dps)]
    delta = jnp.sum(functools.reduce(jnp.add, ts), axis=0, keepdims=True)
    dss = [t - p * delta for p, t in zip(ps, ts)]
    zero = jnp.zeros((BLOCK, BLOCK), F32)
    def spread(v):
        parts = [jnp.where(causal, zero, v[0])] + v[1:] + [jnp.where(causal, v[0], zero)]
        return [p.astype(BF) for p in parts]
    pb = spread(ps); db = spread(dss)
    for t in range(5):
        acc[1, rows_at(t), :] += dot_nn(pb[t], g)
        acc[0, rows_at(t), :] += dot_nn(db[t], q)
    out = functools.reduce(
        jnp.add, [dot_tn(db[t], kv[0, rows_at(t), :]) for t in range(5)]
    )
    cols = pl.ds(pl.multiple_of(hd * HEAD, HEAD), HEAD)
    dq[qrows, cols] = (out * SCALE).astype(BF)


VLIM = 64800
PUT = True
OUT_SHAPE = pltpu.VMEM


def OUT_SPEC():
    return pl.BlockSpec(memory_space=pltpu.VMEM)


def PUT_SPEC():
    return pl.BlockSpec(memory_space=pltpu.VMEM)


def kernel(
    q_hbm, k_hbm, v_hbm, g_hbm, doc_hbm,
    dq_out, dk_out, dv_out,
    kv, qg, first, acc, dq_st, st1, r1, st0, r0, st2, docs,
    doc_sem, kv_sem, z_sem, o_sem, qg_sem, snd, snd0, snd_z, snd_o, snd_o2,
    x1_s, x1_r, x0_s, x0_r, odq_s, odq_r, okv_s, odk_r, odv_r,
):
    seq = lax.axis_index("seq")
    tp = lax.axis_index("tp")
    z, x = seq // 4, seq % 4
    y, c = tp // 2, tp % 2
    side = x % 2
    slot = (x // 2) * 8 + tp
    head = x * 4 + y
    first_plane, last_plane = z == 0, z == PLANES - 1
    up = (((z + 1) % PLANES) * 4 + x, tp)
    down = (((z + PLANES - 1) % PLANES) * 4 + x, tp)
    other = (seq, y * 2 + (1 - c))

    doc_copy = pltpu.make_async_copy(doc_hbm, docs, doc_sem)
    doc_copy.start()

    barrier = pltpu.get_barrier_semaphore()
    xs = [(x + d) % 4 for d in range(4)]
    ys = [(y + d) % 4 for d in range(4)]
    for dx, dy in sorted(
        ((a, b) for a in range(4) for b in range(4)),
        key=lambda p: -(min(p[0], 4 - p[0]) + min(p[1], 4 - p[1])),
    ):
        for tc in (1 - c, c) if (dx, dy) != (0, 0) else (1 - c,):
            pl.semaphore_signal(
                barrier, inc=1, device_id=(z * 4 + xs[dx], ys[dy] * 2 + tc),
                device_id_type=MESH,
            )

    @pl.when(z < PLANES - 1)
    def _():
        pl.semaphore_signal(barrier, inc=1, device_id=up, device_id_type=MESH)

    @pl.when(z > 0)
    def _():
        pl.semaphore_signal(barrier, inc=1, device_id=down, device_id_type=MESH)

    acc[...] = jnp.zeros(acc.shape, F32)

    @pl.when(first_plane)
    def _():
        kv[:, 0:WINDOW, :] = jnp.zeros((2, WINDOW, HEAD), BF)

    @pl.when(last_plane)
    def _():
        r0[...] = jnp.zeros(r0.shape, BF)

    pl.semaphore_wait(barrier, 33 - z // (PLANES - 1) - (PLANES - 1 - z) // (PLANES - 1))

    def key_rows(at):
        return pl.ds(pl.multiple_of(at, ROWS), ROWS)

    def remote(src, dst, send, recv, dev):
        pltpu.make_async_remote_copy(
            src_ref=src, dst_ref=dst, send_sem=send, recv_sem=recv,
            device_id=dev, device_id_type=MESH,
        ).start()

    def bytes_of(ref, sem):
        return pltpu.make_async_copy(ref, ref, sem)

    my_keys = key_rows(WINDOW + x * BLOCK + ROWS * tp)
    my_rows = key_rows(ROWS * slot)

    def in_pairs(h):
        kcols = pl.ds(pl.multiple_of(h * HEAD, HEAD), HEAD)
        pairs = [
            (k_hbm.at[:, kcols], kv.at[0, my_keys, :], kv_sem.at[slot]),
            (v_hbm.at[:, kcols], kv.at[1, my_keys, :], kv_sem.at[slot]),
        ]
        for hd in range(2):
            qcols = pl.ds(pl.multiple_of(h * 2 * HEAD + hd * HEAD, HEAD), HEAD)
            for j, ref in enumerate((q_hbm, g_hbm)):
                pairs.append((ref.at[:, qcols], qg.at[hd, j, my_rows, :], qg_sem.at[hd]))
        return pairs

    def send_here(kinds):
        @pl.when(c == side)
        def _():
            for src, dst, sem in in_pairs(head)[kinds]:
                pltpu.make_async_copy(src, dst, sem).start()

        @pl.when(c != side)
        def _():
            for src, dst, sem in in_pairs(head)[kinds]:
                remote(src, dst, snd0, sem, other)

    def send_away(kinds, i):
        tx = (x + i % 4) % 4
        ty = (y + i % 4 + i // 4) % 4
        for src, dst, sem in in_pairs(tx * 4 + ty)[kinds]:
            remote(src, dst, snd, sem, (z * 4 + tx, ty * 2 + side))

    KEYS, HEAD0, HEAD1 = slice(0, 2), slice(2, 4), slice(4, 6)

    def send_all(kinds):
        def step(i, carry):
            send_away(kinds, i)
            return carry

        lax.fori_loop(1, 16, step, 0)

    send_here(KEYS)
    send_all(KEYS)
    send_here(HEAD0)
    send_all(HEAD0)
    send_here(HEAD1)

    doc_copy.wait()
    for j in range(2):
        begin = z * 1024 + (2 * j + c) * BLOCK
        pos = lax.broadcasted_iota(jnp.int32, (1, BLOCK), 1) + begin
        low = jnp.zeros((1, BLOCK), jnp.int32)
        start = jnp.int32(0)
        for d in range(DOCS):
            low = jnp.where(pos >= start, start, low)
            start = start + docs[d]
        first[:, j * BLOCK : (j + 1) * BLOCK] = low - (z - 1) * 1024

    def source(i):
        half = (i // 2) % 2
        dx = (x + 4 - 2 * half - c) % 4
        sy = (y + 8 - dx - i // 4) % 4
        return half * 8 + sy * 2 + i % 2, (2 * half + c) * BLOCK + ROWS * (sy * 2 + i % 2)

    def relay(i):
        s, at = source(i)
        mine = kv.at[:, key_rows(WINDOW + at), :]
        ahead = kv.at[:, key_rows(at), :]
        bytes_of(mine, kv_sem.at[s]).wait()

        @pl.when(z < PLANES - 1)
        def _():
            remote(mine, ahead, snd_z, z_sem.at[s], up)

        remote(mine, mine, snd_o, o_sem, other)

    relay(0)

    def relay_send(s, carry):
        relay(s)
        send_away(HEAD1, s)
        return carry

    lax.fori_loop(1, 16, relay_send, 0)

    def relay_core(i, carry):
        s, at = source(i)
        mine = kv.at[:, key_rows(at), :]
        bytes_of(mine, z_sem.at[s]).wait()
        remote(mine, mine, snd_o2, o_sem, other)
        return carry

    @pl.when(z > 0)
    def _():
        lax.fori_loop(0, 16, relay_core, 0)
        bytes_of(kv.at[:, 0:WINDOW, :], o_sem).wait()

    @pl.when(first_plane)
    def _():
        bytes_of(kv.at[:, 0:HALF, :], o_sem).wait()

    def run_unit(hd, j):
        at = pl.multiple_of((2 * j + c) * BLOCK, BLOCK)
        if COMPUTE:
            unit(hd, j, at, kv, qg, first, acc, dq_st)

    def tile(t):
        return acc[:, pl.ds(pl.multiple_of(t * BLOCK, BLOCK), BLOCK), :]

    def ship_core(m, t):
        st1[m] = tile(t).astype(BF)
        remote(st1.at[m], r1.at[m], x1_s, x1_r.at[m], other)

    def half_start(h):
        return 128 * ((1 + h + y // 2) % 2)

    def half_rows(h):
        return pl.ds(pl.multiple_of(half_start(h), 128), 128)

    def ship_down(i, total):
        st0[i] = total.astype(BF)

        @pl.when(z > 0)
        def _():
            for h in range(2):
                part = half_rows(h)
                remote(
                    st0.at[i, :, part, :], r0.at[i, :, part, :],
                    x0_s, x0_r.at[2 * i + h], down,
                )

    bytes_of(qg.at[0], qg_sem.at[0]).wait()
    run_unit(0, 0)
    bytes_of(qg.at[1], qg_sem.at[1]).wait()
    run_unit(1, 0)

    ship_core(0, 1 + c)

    @pl.when(c == 0)
    def _():
        ship_down(0, tile(0))

    run_unit(0, 1)

    @pl.when(c == 1)
    def _():
        bytes_of(r1.at[0], x1_r.at[0]).wait()
        ship_down(0, tile(1) + r1[0].astype(F32))

    run_unit(1, 1)

    ship_core(1, 3 + c)

    @pl.when(c == 0)
    def _():
        bytes_of(r1.at[0], x1_r.at[0]).wait()
        ship_down(1, tile(2) + r1[0].astype(F32))

    ship_core(2, 5 + c)
    bytes_of(r1.at[1], x1_r.at[1]).wait()

    @pl.when(c == 1)
    def _():
        ship_down(1, tile(3) + r1[1].astype(F32))

    own = c == side

    def send_out(s, pairs, sem0):
        dev = (z * 4 + 2 * (s // 8) + c, s % 8)
        here = own & (s == slot)

        @pl.when(here)
        def _():
            for src, dst, sem in pairs:
                pltpu.make_async_copy(src, dst, sem).start()

        @pl.when(jnp.logical_not(here))
        def _():
            for src, dst, sem in pairs:
                remote(src, dst, sem0, sem, dev)

    qcols = pl.ds(pl.multiple_of(head * 2 * HEAD, 2 * HEAD), 2 * HEAD)
    kcols = pl.ds(pl.multiple_of(head * HEAD, HEAD), HEAD)

    def dq_step(i, carry):
        s = (slot + i) % 16
        send_out(s, [(dq_st.at[key_rows(ROWS * s), :], dq_out.at[:, qcols], odq_r)], odq_s)
        return carry

    lax.fori_loop(0, 16, dq_step, 0)

    def finish(j, begin, count, extra):
        def span(at):
            return pl.ds(pl.multiple_of(at + begin, 128), count)

        whole = acc[:, span(WINDOW + (2 * j + c) * BLOCK), :]
        whole = whole + r0[j, :, span(0), :].astype(F32)
        if extra is not None:
            whole = whole + extra[:, span(0), :].astype(F32)
        st2[0, span(j * BLOCK), :] = (whole[0] * SCALE).astype(BF)
        st2[1, span(j * BLOCK), :] = whole[1].astype(BF)

        def step(i, carry):
            s = j * 8 + begin // ROWS + i
            send_out(
                s,
                [
                    (st2.at[0, key_rows(ROWS * s), :], dk_out.at[:, kcols], odk_r),
                    (st2.at[1, key_rows(ROWS * s), :], dv_out.at[:, kcols], odv_r),
                ],
                okv_s,
            )
            return carry

        lax.fori_loop(0, count // ROWS, step, 0)

    def await_down(i, h):
        @pl.when(z < PLANES - 1)
        def _():
            bytes_of(r0.at[i, :, half_rows(h), :], x0_r.at[2 * i + h]).wait()

    bytes_of(r1.at[2], x1_r.at[2]).wait()
    await_down(0, 0)
    await_down(0, 1)
    finish(0, 0, BLOCK, r1.at[1 + c])

    @pl.when(c == 0)
    def _():
        acc[:, WINDOW + 2 * BLOCK : WINDOW + 3 * BLOCK, :] += r1[2].astype(F32)

    for h in range(2):
        await_down(1, h)
        finish(1, half_start(h), 128, None)

    bytes_of(kv.at[:, 0:1440, :], snd).wait()

    @pl.when(jnp.logical_not(own))
    def _():
        bytes_of(kv.at[:, 0:96, :], snd0).wait()
        bytes_of(dq_st, odq_s).wait()
        bytes_of(st2, okv_s).wait()

    @pl.when(own)
    def _():
        bytes_of(dq_st.at[0 : HALF - ROWS, :], odq_s).wait()
        bytes_of(st2.at[:, 0 : HALF - ROWS, :], okv_s).wait()

    bytes_of(kv.at[:, 0:HALF, :], snd_o).wait()
    bytes_of(st1, x1_s).wait()

    @pl.when(z < PLANES - 1)
    def _():
        bytes_of(kv.at[:, 0:HALF, :], snd_z).wait()

    @pl.when(z > 0)
    def _():
        bytes_of(kv.at[:, 0:HALF, :], snd_o2).wait()
        bytes_of(st0, x0_s).wait()
    bytes_of(dq_out, odq_r).wait()
    bytes_of(dk_out, odk_r).wait()
    bytes_of(dv_out, odv_r).wait()


def put_kernel(a, b, d, oa, ob, od, sem):
    copies = [
        pltpu.make_async_copy(src, dst, sem.at[i])
        for i, (src, dst) in enumerate(((a, oa), (b, ob), (d, od)))
    ]
    for copy in copies:
        copy.start()
    for copy in copies:
        copy.wait()


def per_device(queries, key_states, value_state_rows, out_grad, doc_lengths):
    any_space = pl.BlockSpec(memory_space=pl.ANY)
    vmem_space = pl.BlockSpec(memory_space=pltpu.VMEM)
    dma = pltpu.SemaphoreType.DMA
    shapes = [queries.shape, key_states.shape, value_state_rows.shape]
    results = pl.pallas_call(
        kernel,
        out_shape=tuple(OUT_SHAPE(s, BF) for s in shapes),
        in_specs=[pl.BlockSpec(memory_space=pltpu.HBM)] * 5,
        out_specs=(OUT_SPEC(),) * 3,
        scratch_shapes=[
            pltpu.VMEM((2, 2 * WINDOW, HEAD), BF),
            pltpu.VMEM((2, 2, HALF, HEAD), BF),
            pltpu.VMEM((1, HALF), jnp.int32),
            pltpu.VMEM((2, 2 * WINDOW, HEAD), F32),
            pltpu.VMEM((HALF, 2 * HEAD), BF),
            pltpu.VMEM((3, 2, BLOCK, HEAD), BF),
            pltpu.VMEM((3, 2, BLOCK, HEAD), BF),
            pltpu.VMEM((2, 2, BLOCK, HEAD), BF),
            pltpu.VMEM((2, 2, BLOCK, HEAD), BF),
            pltpu.VMEM((2, HALF, HEAD), BF),
            pltpu.SMEM((DOCS,), jnp.int32),
            dma, dma((16,)), dma((16,)), dma, dma((2,)), dma, dma, dma, dma, dma,
            dma, dma((3,)), dma, dma((4,)), dma, dma, dma, dma, dma,
        ],
        compiler_params=pltpu.CompilerParams(
            collective_id=0, has_side_effects=True, vmem_limit_bytes=VLIM * 1024
        ),
        name="window_attention_backward",
    )(queries, key_states, value_state_rows, out_grad, doc_lengths)
    if not PUT:
        return results
    return pl.pallas_call(
        put_kernel,
        out_shape=tuple(jax.ShapeDtypeStruct(s, BF) for s in shapes),
        in_specs=[PUT_SPEC()] * 3,
        out_specs=(any_space,) * 3,
        scratch_shapes=[dma((3,))],
        compiler_params=pltpu.CompilerParams(vmem_limit_bytes=1024 * 1024),
        name="put_results",
    )(*results)


COMPUTE = True


def solution(mesh):
    rows = P(("seq", "tp"), None)
    return jax.shard_map(
        per_device,
        mesh=mesh,
        in_specs=(rows, rows, rows, rows, P()),
        out_specs=(rows, rows, rows),
        check_vma=False,
    )
```

```python
import functools
import math

import jax
import jax.numpy as jnp
from jax import lax
from jax.experimental import pallas as pl
from jax.experimental.pallas import tpu as pltpu
from jax.sharding import PartitionSpec as P

MESH = pl.DeviceIdType.MESH
HEAD = 128
ROWS = 32
HALF = 512
BLOCK = 256
SPAN = 3 * HALF
WINDOW = 1024
DOCS = 16
PLANES = 16
SCALE = 168.0 ** (-0.5)
EXP_SCALE = SCALE / math.log(2.0)
FLOOR = -1e30
BF = jnp.bfloat16
F32 = jnp.float32


def dot_nt(a, b):
    return lax.dot_general(a, b, (((1,), (1,)), ((), ())), preferred_element_type=F32)


def dot_nn(a, b):
    return lax.dot_general(a, b, (((1,), (0,)), ((), ())), preferred_element_type=F32)


def dot_tn(a, b):
    return lax.dot_general(a, b, (((0,), (0,)), ((), ())), preferred_element_type=F32)


def unit(hd, j, at, kv, qg, first, acc, dq):
    qrows = pl.ds(pl.multiple_of(j * BLOCK, BLOCK), BLOCK)
    q = qg[hd, 0, qrows, :]
    g = qg[hd, 1, qrows, :]
    low = first[:, qrows] - at
    row = lax.broadcasted_iota(jnp.int32, (BLOCK, BLOCK), 0)
    col = lax.broadcasted_iota(jnp.int32, (BLOCK, BLOCK), 1)
    causal = row <= col
    def rows_at(t):
        return pl.ds(pl.multiple_of(at + t * BLOCK, BLOCK), BLOCK)
    def tiles_of(which, w):
        far = dot_nt(kv[which, rows_at(0), :], w)
        near = dot_nt(kv[which, rows_at(4), :], w)
        return [jnp.where(causal, near, far)] + [dot_nt(kv[which, rows_at(t), :], w) for t in (1, 2, 3)]
    scores = tiles_of(0, q)
    scores = [jnp.where(jnp.where(causal, row + 4 * BLOCK, row) >= low, scores[0], FLOOR)] + [
        jnp.where(row >= low - t * BLOCK, scores[t], FLOOR) for t in (1, 2, 3)]
    peak = functools.reduce(jnp.maximum, scores)
    peak = jnp.max(peak, axis=0, keepdims=True) * EXP_SCALE
    ps = [jnp.exp2(s * EXP_SCALE - peak) for s in scores]
    total = jnp.sum(functools.reduce(jnp.add, ps), axis=0, keepdims=True)
    inverse = 1.0 / total
    dps = tiles_of(1, g)
    ps = [p * inverse for p in ps]
    ts = [p * d for p, d in zip(ps, dps)]
    delta = jnp.sum(functools.reduce(jnp.add, ts), axis=0, keepdims=True)
    dss = [t - p * delta for p, t in zip(ps, ts)]
    zero = jnp.zeros((BLOCK, BLOCK), F32)
    def spread(v):
        parts = [jnp.where(causal, zero, v[0])] + v[1:] + [jnp.where(causal, v[0], zero)]
        return [p.astype(BF) for p in parts]
    pb = spread(ps); db = spread(dss)
    for t in range(5):
        acc[1, rows_at(t), :] += dot_nn(pb[t], g)
        acc[0, rows_at(t), :] += dot_nn(db[t], q)
    out = functools.reduce(
        jnp.add, [dot_tn(db[t], kv[0, rows_at(t), :]) for t in range(5)]
    )
    cols = pl.ds(pl.multiple_of(hd * HEAD, HEAD), HEAD)
    dq[qrows, cols] = (out * SCALE).astype(BF)


VLIM = 64800
PUT = True
OUT_SHAPE = pltpu.VMEM


def OUT_SPEC():
    return pl.BlockSpec(memory_space=pltpu.VMEM)


def PUT_SPEC():
    return pl.BlockSpec(memory_space=pltpu.VMEM)


def kernel(
    q_hbm, k_hbm, v_hbm, g_hbm, doc_hbm,
    dq_out, dk_out, dv_out,
    kv, qg, first, acc, dq_st, st1, r1, st0, r0, st2, docs,
    doc_sem, root_sem, kv_sem, z_sem, o_sem, qg_sem, snd, snd0, snd_z, snd_o, snd_o2,
    x1_s, x1_r, x0_s, x0_r, odq_s, odq_r, okv_s, odk_r, odv_r,
):
    seq = lax.axis_index("seq")
    tp = lax.axis_index("tp")
    z, x = seq // 4, seq % 4
    y, c = tp // 2, tp % 2
    side = x % 2
    slot = (x // 2) * 8 + tp
    head = x * 4 + y
    first_plane, last_plane = z == 0, z == PLANES - 1
    up = (((z + 1) % PLANES) * 4 + x, tp)
    down = (((z + PLANES - 1) % PLANES) * 4 + x, tp)
    other = (seq, y * 2 + (1 - c))

    doc_copy = pltpu.make_async_copy(doc_hbm, docs, doc_sem)
    doc_copy.start()

    barrier = pltpu.get_barrier_semaphore()
    xs = [(x + d) % 4 for d in range(4)]
    ys = [(y + d) % 4 for d in range(4)]

    def greet(sem):
        for dx, dy in sorted(
            ((a, b) for a in range(4) for b in range(4)),
            key=lambda p: -(min(p[0], 4 - p[0]) + min(p[1], 4 - p[1])),
        ):
            for tc in (1 - c, c) if (dx, dy) != (0, 0) else (1 - c,):
                pl.semaphore_signal(
                    sem, inc=1, device_id=(z * 4 + xs[dx], ys[dy] * 2 + tc),
                    device_id_type=MESH,
                )

    root = (seq == 0) & (tp == 0)
    beside_root = (z == 0) & jnp.logical_not(root)

    @pl.when(jnp.logical_not(root))
    def _():
        greet(barrier)

    @pl.when(z < PLANES - 1)
    def _():
        pl.semaphore_signal(barrier, inc=1, device_id=up, device_id_type=MESH)

    @pl.when(z > 0)
    def _():
        pl.semaphore_signal(barrier, inc=1, device_id=down, device_id_type=MESH)

    acc[...] = jnp.zeros(acc.shape, F32)

    @pl.when(first_plane)
    def _():
        kv[:, 0:WINDOW, :] = jnp.zeros((2, WINDOW, HEAD), BF)

    @pl.when(last_plane)
    def _():
        r0[...] = jnp.zeros(r0.shape, BF)

    in_first = (PLANES - 1 - z) // (PLANES - 1)
    is_root = in_first * ((3 - x) // 3) * ((7 - tp) // 7)
    pl.semaphore_wait(barrier, 33 - z // (PLANES - 1) - 2 * in_first + is_root)

    @pl.when(root)
    def _():
        greet(root_sem)

    def key_rows(at):
        return pl.ds(pl.multiple_of(at, ROWS), ROWS)

    def remote(src, dst, send, recv, dev):
        pltpu.make_async_remote_copy(
            src_ref=src, dst_ref=dst, send_sem=send, recv_sem=recv,
            device_id=dev, device_id_type=MESH,
        ).start()

    def bytes_of(ref, sem):
        return pltpu.make_async_copy(ref, ref, sem)

    my_keys = key_rows(WINDOW + x * BLOCK + ROWS * tp)
    my_rows = key_rows(ROWS * slot)

    def in_pairs(h):
        kcols = pl.ds(pl.multiple_of(h * HEAD, HEAD), HEAD)
        pairs = [
            (k_hbm.at[:, kcols], kv.at[0, my_keys, :], kv_sem.at[slot]),
            (v_hbm.at[:, kcols], kv.at[1, my_keys, :], kv_sem.at[slot]),
        ]
        for hd in range(2):
            qcols = pl.ds(pl.multiple_of(h * 2 * HEAD + hd * HEAD, HEAD), HEAD)
            for j, ref in enumerate((q_hbm, g_hbm)):
                pairs.append((ref.at[:, qcols], qg.at[hd, j, my_rows, :], qg_sem.at[hd]))
        return pairs

    def send_here(kinds):
        @pl.when(c == side)
        def _():
            for src, dst, sem in in_pairs(head)[kinds]:
                pltpu.make_async_copy(src, dst, sem).start()

        @pl.when((c != side) & jnp.logical_not(beside_root & (head == 0) & (side == 0)))
        def _():
            for src, dst, sem in in_pairs(head)[kinds]:
                remote(src, dst, snd0, sem, other)

    def send_away(kinds, i):
        tx = (x + i % 4) % 4
        ty = (y + i % 4 + i // 4) % 4
        for src, dst, sem in in_pairs(tx * 4 + ty)[kinds]:
            remote(src, dst, snd, sem, (z * 4 + tx, ty * 2 + side))

    def send_early(kinds, i):
        tx = (x + i % 4) % 4
        ty = (y + i % 4 + i // 4) % 4

        @pl.when(jnp.logical_not((z == 0) & (tx == 0) & (ty == 0) & (side == 0)))
        def _():
            for src, dst, sem in in_pairs(tx * 4 + ty)[kinds]:
                remote(src, dst, snd, sem, (z * 4 + tx, ty * 2 + side))

    KEYS, HEAD0, HEAD1 = slice(0, 2), slice(2, 4), slice(4, 6)

    def send_all(kinds):
        def step(i, carry):
            send_early(kinds, i)
            return carry

        lax.fori_loop(1, 16, step, 0)

    send_here(KEYS)
    send_all(KEYS)
    send_here(HEAD0)
    send_all(HEAD0)
    send_here(HEAD1)

    @pl.when(beside_root)
    def _():
        pl.semaphore_wait(root_sem, 1)

        @pl.when((side == 0) & (head != 0))
        def _():
            for src, dst, sem in in_pairs(0)[0:4]:
                remote(src, dst, snd, sem, (0, 0))

        @pl.when((side == 0) & (head == 0))
        def _():
            for src, dst, sem in in_pairs(0):
                remote(src, dst, snd0, sem, (0, 0))

    doc_copy.wait()
    for j in range(2):
        begin = z * 1024 + (2 * j + c) * BLOCK
        pos = lax.broadcasted_iota(jnp.int32, (1, BLOCK), 1) + begin
        low = jnp.zeros((1, BLOCK), jnp.int32)
        start = jnp.int32(0)
        for d in range(DOCS):
            low = jnp.where(pos >= start, start, low)
            start = start + docs[d]
        first[:, j * BLOCK : (j + 1) * BLOCK] = low - (z - 1) * 1024

    def source(i):
        half = (i // 2) % 2
        dx = (x + 4 - 2 * half - c) % 4
        sy = (y + 8 - dx - i // 4) % 4
        return half * 8 + sy * 2 + i % 2, (2 * half + c) * BLOCK + ROWS * (sy * 2 + i % 2)

    def relay(i):
        s, at = source(i)
        mine = kv.at[:, key_rows(WINDOW + at), :]
        ahead = kv.at[:, key_rows(at), :]
        bytes_of(mine, kv_sem.at[s]).wait()

        @pl.when(z < PLANES - 1)
        def _():
            remote(mine, ahead, snd_z, z_sem.at[s], up)

        remote(mine, mine, snd_o, o_sem, other)

    relay(0)

    def relay_send(s, carry):
        relay(s)
        send_away(HEAD1, s)
        return carry

    lax.fori_loop(1, 16, relay_send, 0)

    def relay_core(i, carry):
        s, at = source(i)
        mine = kv.at[:, key_rows(at), :]
        bytes_of(mine, z_sem.at[s]).wait()
        remote(mine, mine, snd_o2, o_sem, other)
        return carry

    @pl.when(z > 0)
    def _():
        lax.fori_loop(0, 16, relay_core, 0)
        bytes_of(kv.at[:, 0:WINDOW, :], o_sem).wait()

    @pl.when(first_plane)
    def _():
        bytes_of(kv.at[:, 0:HALF, :], o_sem).wait()

    def run_unit(hd, j):
        at = pl.multiple_of((2 * j + c) * BLOCK, BLOCK)
        unit(hd, j, at, kv, qg, first, acc, dq_st)

    def tile(t):
        return acc[:, pl.ds(pl.multiple_of(t * BLOCK, BLOCK), BLOCK), :]

    def ship_core(m, t):
        st1[m] = tile(t).astype(BF)
        remote(st1.at[m], r1.at[m], x1_s, x1_r.at[m], other)

    def half_start(h):
        return 128 * ((1 + h + y // 2) % 2)

    def half_rows(h):
        return pl.ds(pl.multiple_of(half_start(h), 128), 128)

    def send_down(i, h):
        @pl.when(z > 0)
        def _():
            part = half_rows(h)
            remote(
                st0.at[i, :, part, :], r0.at[i, :, part, :],
                x0_s, x0_r.at[2 * i + h], down,
            )

    def ship_down(i, total, halves):
        st0[i] = total.astype(BF)
        for h in halves:
            send_down(i, h)

    bytes_of(qg.at[0], qg_sem.at[0]).wait()
    run_unit(0, 0)
    bytes_of(qg.at[1], qg_sem.at[1]).wait()
    run_unit(1, 0)

    ship_core(0, 1 + c)

    @pl.when(c == 0)
    def _():
        ship_down(0, tile(0), (0, 1))

    run_unit(0, 1)

    @pl.when(c == 1)
    def _():
        bytes_of(r1.at[0], x1_r.at[0]).wait()
        ship_down(0, tile(1) + r1[0].astype(F32), (0, 1))

    run_unit(1, 1)

    ship_core(1, 3 + c)

    @pl.when(c == 0)
    def _():
        bytes_of(r1.at[0], x1_r.at[0]).wait()
        ship_down(1, tile(2) + r1[0].astype(F32), (0,))

    own = c == side

    def send_out(s, pairs, sem0):
        dev = (z * 4 + 2 * (s // 8) + c, s % 8)
        here = own & (s == slot)

        @pl.when(here)
        def _():
            for src, dst, sem in pairs:
                pltpu.make_async_copy(src, dst, sem).start()

        @pl.when(jnp.logical_not(here))
        def _():
            for src, dst, sem in pairs:
                remote(src, dst, sem0, sem, dev)

    qcols = pl.ds(pl.multiple_of(head * 2 * HEAD, 2 * HEAD), 2 * HEAD)
    kcols = pl.ds(pl.multiple_of(head * HEAD, HEAD), HEAD)

    def dq_step(i, carry):
        s = (slot + i) % 16
        send_out(s, [(dq_st.at[key_rows(ROWS * s), :], dq_out.at[:, qcols], odq_r)], odq_s)
        return carry

    lax.fori_loop(0, 8, dq_step, 0)

    @pl.when(c == 1)
    def _():
        bytes_of(r1.at[1], x1_r.at[1]).wait()
        ship_down(1, tile(3) + r1[1].astype(F32), (0,))

    lax.fori_loop(8, 16, dq_step, 0)
    send_down(1, 1)
    ship_core(2, 5 + c)

    @pl.when(c == 0)
    def _():
        bytes_of(r1.at[1], x1_r.at[1]).wait()

    def finish(j, begin, count, extra):
        def span(at):
            return pl.ds(pl.multiple_of(at + begin, 128), count)

        whole = acc[:, span(WINDOW + (2 * j + c) * BLOCK), :]
        whole = whole + r0[j, :, span(0), :].astype(F32)
        if extra is not None:
            whole = whole + extra[:, span(0), :].astype(F32)
        st2[0, span(j * BLOCK), :] = (whole[0] * SCALE).astype(BF)
        st2[1, span(j * BLOCK), :] = whole[1].astype(BF)

        def step(i, carry):
            s = j * 8 + begin // ROWS + i
            send_out(
                s,
                [
                    (st2.at[0, key_rows(ROWS * s), :], dk_out.at[:, kcols], odk_r),
                    (st2.at[1, key_rows(ROWS * s), :], dv_out.at[:, kcols], odv_r),
                ],
                okv_s,
            )
            return carry

        lax.fori_loop(0, count // ROWS, step, 0)

    def await_down(i, h):
        @pl.when(z < PLANES - 1)
        def _():
            bytes_of(r0.at[i, :, half_rows(h), :], x0_r.at[2 * i + h]).wait()

    bytes_of(r1.at[2], x1_r.at[2]).wait()
    await_down(0, 0)
    await_down(0, 1)
    finish(0, 0, BLOCK, r1.at[1 + c])

    @pl.when(c == 0)
    def _():
        acc[:, WINDOW + 2 * BLOCK : WINDOW + 3 * BLOCK, :] += r1[2].astype(F32)

    for h in range(2):
        await_down(1, h)
        finish(1, half_start(h), 128, None)

    bytes_of(kv.at[:, 0:1440, :], snd).wait()

    @pl.when(jnp.logical_not(own))
    def _():
        bytes_of(kv.at[:, 0:96, :], snd0).wait()
        bytes_of(dq_st, odq_s).wait()
        bytes_of(st2, okv_s).wait()

    @pl.when(own)
    def _():
        bytes_of(dq_st.at[0 : HALF - ROWS, :], odq_s).wait()
        bytes_of(st2.at[:, 0 : HALF - ROWS, :], okv_s).wait()

    bytes_of(kv.at[:, 0:HALF, :], snd_o).wait()
    bytes_of(st1, x1_s).wait()

    @pl.when(z < PLANES - 1)
    def _():
        bytes_of(kv.at[:, 0:HALF, :], snd_z).wait()

    @pl.when(z > 0)
    def _():
        bytes_of(kv.at[:, 0:HALF, :], snd_o2).wait()
        bytes_of(st0, x0_s).wait()
    bytes_of(dq_out, odq_r).wait()
    bytes_of(dk_out, odk_r).wait()
    bytes_of(dv_out, odv_r).wait()


def put_kernel(a, b, d, oa, ob, od, sem):
    copies = [
        pltpu.make_async_copy(src, dst, sem.at[i])
        for i, (src, dst) in enumerate(((a, oa), (b, ob), (d, od)))
    ]
    for copy in copies:
        copy.start()
    for copy in copies:
        copy.wait()


def per_device(queries, key_states, value_state_rows, out_grad, doc_lengths):
    any_space = pl.BlockSpec(memory_space=pl.ANY)
    vmem_space = pl.BlockSpec(memory_space=pltpu.VMEM)
    dma = pltpu.SemaphoreType.DMA
    shapes = [queries.shape, key_states.shape, value_state_rows.shape]
    results = pl.pallas_call(
        kernel,
        out_shape=tuple(OUT_SHAPE(s, BF) for s in shapes),
        in_specs=[pl.BlockSpec(memory_space=pltpu.HBM)] * 5,
        out_specs=(OUT_SPEC(),) * 3,
        scratch_shapes=[
            pltpu.VMEM((2, 2 * WINDOW, HEAD), BF),
            pltpu.VMEM((2, 2, HALF, HEAD), BF),
            pltpu.VMEM((1, HALF), jnp.int32),
            pltpu.VMEM((2, 2 * WINDOW, HEAD), F32),
            pltpu.VMEM((HALF, 2 * HEAD), BF),
            pltpu.VMEM((3, 2, BLOCK, HEAD), BF),
            pltpu.VMEM((3, 2, BLOCK, HEAD), BF),
            pltpu.VMEM((2, 2, BLOCK, HEAD), BF),
            pltpu.VMEM((2, 2, BLOCK, HEAD), BF),
            pltpu.VMEM((2, HALF, HEAD), BF),
            pltpu.SMEM((DOCS,), jnp.int32),
            dma, pltpu.SemaphoreType.REGULAR, dma((16,)), dma((16,)), dma, dma((2,)), dma, dma, dma, dma, dma,
            dma, dma((3,)), dma, dma((4,)), dma, dma, dma, dma, dma,
        ],
        compiler_params=pltpu.CompilerParams(
            collective_id=0, has_side_effects=True, vmem_limit_bytes=VLIM * 1024
        ),
        name="window_attention_backward",
    )(queries, key_states, value_state_rows, out_grad, doc_lengths)
    if not PUT:
        return results
    return pl.pallas_call(
        put_kernel,
        out_shape=tuple(jax.ShapeDtypeStruct(s, BF) for s in shapes),
        in_specs=[PUT_SPEC()] * 3,
        out_specs=(any_space,) * 3,
        scratch_shapes=[dma((3,))],
        compiler_params=pltpu.CompilerParams(vmem_limit_bytes=1024 * 1024),
        name="put_results",
    )(*results)


def solution(mesh):
    rows = P(("seq", "tp"), None)
    return jax.shard_map(
        per_device,
        mesh=mesh,
        in_specs=(rows, rows, rows, rows, P()),
        out_specs=(rows, rows, rows),
        check_vma=False,
    )
```

```python
import functools
import math

import jax
import jax.numpy as jnp
from jax import lax
from jax.experimental import pallas as pl
from jax.experimental.pallas import tpu as pltpu
from jax.sharding import PartitionSpec as P

MESH = pl.DeviceIdType.MESH
HEAD = 128
ROWS = 32
HALF = 512
BLOCK = 256
SPAN = 3 * HALF
WINDOW = 1024
DOCS = 16
PLANES = 16
SCALE = 168.0 ** (-0.5)
EXP_SCALE = SCALE / math.log(2.0)
FLOOR = -1e30
BF = jnp.bfloat16
F32 = jnp.float32


def dot_nt(a, b):
    return lax.dot_general(a, b, (((1,), (1,)), ((), ())), preferred_element_type=F32)


def dot_nn(a, b):
    return lax.dot_general(a, b, (((1,), (0,)), ((), ())), preferred_element_type=F32)


def dot_tn(a, b):
    return lax.dot_general(a, b, (((0,), (0,)), ((), ())), preferred_element_type=F32)


def unit(hd, j, at, kv, qg, first, acc, dq):
    qrows = pl.ds(pl.multiple_of(j * BLOCK, BLOCK), BLOCK)
    q = qg[hd, 0, qrows, :]
    g = qg[hd, 1, qrows, :]
    low = first[:, qrows] - at
    row = lax.broadcasted_iota(jnp.int32, (BLOCK, BLOCK), 0)
    col = lax.broadcasted_iota(jnp.int32, (BLOCK, BLOCK), 1)
    causal = row <= col
    def rows_at(t):
        return pl.ds(pl.multiple_of(at + t * BLOCK, BLOCK), BLOCK)
    def tiles_of(which, w):
        far = dot_nt(kv[which, rows_at(0), :], w)
        near = dot_nt(kv[which, rows_at(4), :], w)
        return [jnp.where(causal, near, far)] + [dot_nt(kv[which, rows_at(t), :], w) for t in (1, 2, 3)]
    scores = tiles_of(0, q)
    scores = [jnp.where(jnp.where(causal, row + 4 * BLOCK, row) >= low, scores[0], FLOOR)] + [
        jnp.where(row >= low - t * BLOCK, scores[t], FLOOR) for t in (1, 2, 3)]
    peak = functools.reduce(jnp.maximum, scores)
    peak = jnp.max(peak, axis=0, keepdims=True) * EXP_SCALE
    ps = [jnp.exp2(s * EXP_SCALE - peak) for s in scores]
    total = jnp.sum(functools.reduce(jnp.add, ps), axis=0, keepdims=True)
    inverse = 1.0 / total
    dps = tiles_of(1, g)
    ps = [p * inverse for p in ps]
    ts = [p * d for p, d in zip(ps, dps)]
    delta = jnp.sum(functools.reduce(jnp.add, ts), axis=0, keepdims=True)
    dss = [t - p * delta for p, t in zip(ps, ts)]
    zero = jnp.zeros((BLOCK, BLOCK), F32)
    def spread(v):
        parts = [jnp.where(causal, zero, v[0])] + v[1:] + [jnp.where(causal, v[0], zero)]
        return [p.astype(BF) for p in parts]
    pb = spread(ps); db = spread(dss)
    for t in range(5):
        acc[1, rows_at(t), :] += dot_nn(pb[t], g)
        acc[0, rows_at(t), :] += dot_nn(db[t], q)
    out = functools.reduce(
        jnp.add, [dot_tn(db[t], kv[0, rows_at(t), :]) for t in range(5)]
    )
    cols = pl.ds(pl.multiple_of(hd * HEAD, HEAD), HEAD)
    dq[qrows, cols] = (out * SCALE).astype(BF)


VLIM = 64800
PUT = True
OUT_SHAPE = pltpu.VMEM


def OUT_SPEC():
    return pl.BlockSpec(memory_space=pltpu.VMEM)


def PUT_SPEC():
    return pl.BlockSpec(memory_space=pltpu.VMEM)


def kernel(
    q_hbm, k_hbm, v_hbm, g_hbm, doc_hbm,
    dq_out, dk_out, dv_out,
    kv, qg, first, acc, dq_st, st1, r1, st0, r0, st2, docs,
    doc_sem, root_sem, kv_sem, z_sem, o_sem, qg_sem, snd, snd0, snd_z, snd_o, snd_o2,
    x1_s, x1_r, x0_s, x0_r, odq_s, odq_r, okv_s, odk_r, odv_r,
):
    seq = lax.axis_index("seq")
    tp = lax.axis_index("tp")
    z, x = seq // 4, seq % 4
    y, c = tp // 2, tp % 2
    side = x % 2
    slot = (x // 2) * 8 + tp
    head = x * 4 + y
    first_plane, last_plane = z == 0, z == PLANES - 1
    up = (((z + 1) % PLANES) * 4 + x, tp)
    down = (((z + PLANES - 1) % PLANES) * 4 + x, tp)
    other = (seq, y * 2 + (1 - c))

    doc_copy = pltpu.make_async_copy(doc_hbm, docs, doc_sem)
    doc_copy.start()

    barrier = pltpu.get_barrier_semaphore()
    xs = [(x + d) % 4 for d in range(4)]
    ys = [(y + d) % 4 for d in range(4)]

    def greet(sem):
        for dx, dy in sorted(
            ((a, b) for a in range(4) for b in range(4)),
            key=lambda p: -(min(p[0], 4 - p[0]) + min(p[1], 4 - p[1])),
        ):
            for tc in (1 - c, c) if (dx, dy) != (0, 0) else (1 - c,):
                pl.semaphore_signal(
                    sem, inc=1, device_id=(z * 4 + xs[dx], ys[dy] * 2 + tc),
                    device_id_type=MESH,
                )

    root = (seq == 0) & (tp == 0)
    beside_root = (z == 0) & jnp.logical_not(root)

    @pl.when(jnp.logical_not(root))
    def _():
        greet(barrier)

    @pl.when(z < PLANES - 1)
    def _():
        pl.semaphore_signal(barrier, inc=1, device_id=up, device_id_type=MESH)

    @pl.when(z > 0)
    def _():
        pl.semaphore_signal(barrier, inc=1, device_id=down, device_id_type=MESH)

    acc[...] = jnp.zeros(acc.shape, F32)

    @pl.when(first_plane)
    def _():
        kv[:, 0:WINDOW, :] = jnp.zeros((2, WINDOW, HEAD), BF)

    @pl.when(last_plane)
    def _():
        r0[...] = jnp.zeros(r0.shape, BF)

    in_first = (PLANES - 1 - z) // (PLANES - 1)
    is_root = in_first * ((3 - x) // 3) * ((7 - tp) // 7)
    pl.semaphore_wait(barrier, 33 - z // (PLANES - 1) - 2 * in_first + is_root)

    @pl.when(root)
    def _():
        greet(root_sem)

    def key_rows(at):
        return pl.ds(pl.multiple_of(at, ROWS), ROWS)

    def remote(src, dst, send, recv, dev):
        pltpu.make_async_remote_copy(
            src_ref=src, dst_ref=dst, send_sem=send, recv_sem=recv,
            device_id=dev, device_id_type=MESH,
        ).start()

    def bytes_of(ref, sem):
        return pltpu.make_async_copy(ref, ref, sem)

    my_keys = key_rows(WINDOW + x * BLOCK + ROWS * tp)
    my_rows = key_rows(ROWS * slot)

    def in_pairs(h):
        kcols = pl.ds(pl.multiple_of(h * HEAD, HEAD), HEAD)
        pairs = [
            (k_hbm.at[:, kcols], kv.at[0, my_keys, :], kv_sem.at[slot]),
            (v_hbm.at[:, kcols], kv.at[1, my_keys, :], kv_sem.at[slot]),
        ]
        for hd in range(2):
            qcols = pl.ds(pl.multiple_of(h * 2 * HEAD + hd * HEAD, HEAD), HEAD)
            for j, ref in enumerate((q_hbm, g_hbm)):
                pairs.append((ref.at[:, qcols], qg.at[hd, j, my_rows, :], qg_sem.at[hd]))
        return pairs

    def send_here(kinds):
        @pl.when(c == side)
        def _():
            for src, dst, sem in in_pairs(head)[kinds]:
                pltpu.make_async_copy(src, dst, sem).start()

        @pl.when((c != side) & jnp.logical_not(beside_root & (head == 0) & (side == 0)))
        def _():
            for src, dst, sem in in_pairs(head)[kinds]:
                remote(src, dst, snd0, sem, other)

    def send_away(kinds, i):
        tx = (x + i % 4) % 4
        ty = (y + i % 4 + i // 4) % 4
        for src, dst, sem in in_pairs(tx * 4 + ty)[kinds]:
            remote(src, dst, snd, sem, (z * 4 + tx, ty * 2 + side))

    def send_early(kinds, i):
        tx = (x + i % 4) % 4
        ty = (y + i % 4 + i // 4) % 4

        @pl.when(jnp.logical_not((z == 0) & (tx == 0) & (ty == 0) & (side == 0)))
        def _():
            for src, dst, sem in in_pairs(tx * 4 + ty)[kinds]:
                remote(src, dst, snd, sem, (z * 4 + tx, ty * 2 + side))

    KEYS, HEAD0, HEAD1 = slice(0, 2), slice(2, 4), slice(4, 6)

    def send_all(kinds):
        def step(i, carry):
            send_early(kinds, i)
            return carry

        lax.fori_loop(1, 16, step, 0)

    send_here(KEYS)
    send_all(KEYS)
    send_here(HEAD0)
    send_all(HEAD0)
    send_here(HEAD1)

    @pl.when(beside_root)
    def _():
        pl.semaphore_wait(root_sem, 1)

        @pl.when((side == 0) & (head != 0))
        def _():
            for src, dst, sem in in_pairs(0)[0:4]:
                remote(src, dst, snd, sem, (0, 0))

        @pl.when((side == 0) & (head == 0))
        def _():
            for src, dst, sem in in_pairs(0):
                remote(src, dst, snd0, sem, (0, 0))

    doc_copy.wait()
    for j in range(2):
        begin = z * 1024 + (2 * j + c) * BLOCK
        pos = lax.broadcasted_iota(jnp.int32, (1, BLOCK), 1) + begin
        low = jnp.zeros((1, BLOCK), jnp.int32)
        start = jnp.int32(0)
        for d in range(DOCS):
            low = jnp.where(pos >= start, start, low)
            start = start + docs[d]
        first[:, j * BLOCK : (j + 1) * BLOCK] = low - (z - 1) * 1024

    def source(i):
        half = (i // 2) % 2
        dx = (x + 4 - 2 * half - c) % 4
        sy = (y + 8 - dx - i // 4) % 4
        return half * 8 + sy * 2 + i % 2, (2 * half + c) * BLOCK + ROWS * (sy * 2 + i % 2)

    def relay(i):
        s, at = source(i)
        mine = kv.at[:, key_rows(WINDOW + at), :]
        ahead = kv.at[:, key_rows(at), :]
        bytes_of(mine, kv_sem.at[s]).wait()

        @pl.when(z < PLANES - 1)
        def _():
            remote(mine, ahead, snd_z, z_sem.at[s], up)

        remote(mine, mine, snd_o, o_sem, other)

    relay(0)

    def relay_send(s, carry):
        relay(s)
        send_away(HEAD1, s)
        return carry

    lax.fori_loop(1, 16, relay_send, 0)

    def relay_core(i, carry):
        s, at = source(i)
        mine = kv.at[:, key_rows(at), :]
        bytes_of(mine, z_sem.at[s]).wait()
        remote(mine, mine, snd_o2, o_sem, other)
        return carry

    @pl.when(z > 0)
    def _():
        lax.fori_loop(0, 16, relay_core, 0)
        bytes_of(kv.at[:, 0:WINDOW, :], o_sem).wait()

    @pl.when(first_plane)
    def _():
        bytes_of(kv.at[:, 0:HALF, :], o_sem).wait()

    def run_unit(hd, j):
        at = pl.multiple_of((2 * j + c) * BLOCK, BLOCK)
        unit(hd, j, at, kv, qg, first, acc, dq_st)

    def tile(t):
        return acc[:, pl.ds(pl.multiple_of(t * BLOCK, BLOCK), BLOCK), :]

    def ship_core(m, t):
        st1[m] = tile(t).astype(BF)
        remote(st1.at[m], r1.at[m], x1_s, x1_r.at[m], other)

    def half_start(h):
        return 128 * ((1 + h + y // 2) % 2)

    def half_rows(h):
        return pl.ds(pl.multiple_of(half_start(h), 128), 128)

    def send_down(i, h):
        @pl.when(z > 0)
        def _():
            part = half_rows(h)
            remote(
                st0.at[i, :, part, :], r0.at[i, :, part, :],
                x0_s, x0_r.at[2 * i + h], down,
            )

    def ship_down(i, total, halves):
        st0[i] = total.astype(BF)
        for h in halves:
            send_down(i, h)

    bytes_of(qg.at[0], qg_sem.at[0]).wait()
    run_unit(0, 0)
    bytes_of(qg.at[1], qg_sem.at[1]).wait()
    run_unit(1, 0)

    ship_core(0, 1 + c)

    @pl.when(c == 0)
    def _():
        ship_down(0, tile(0), (0, 1))

    run_unit(0, 1)

    @pl.when(c == 1)
    def _():
        bytes_of(r1.at[0], x1_r.at[0]).wait()
        ship_down(0, tile(1) + r1[0].astype(F32), (0, 1))

    run_unit(1, 1)

    ship_core(1, 3 + c)

    @pl.when(c == 0)
    def _():
        bytes_of(r1.at[0], x1_r.at[0]).wait()
        ship_down(1, tile(2) + r1[0].astype(F32), (0,))

    own = c == side

    def send_out(s, pairs, sem0):
        dev = (z * 4 + 2 * (s // 8) + c, s % 8)
        here = own & (s == slot)

        @pl.when(here)
        def _():
            for src, dst, sem in pairs:
                pltpu.make_async_copy(src, dst, sem).start()

        @pl.when(jnp.logical_not(here))
        def _():
            for src, dst, sem in pairs:
                remote(src, dst, sem0, sem, dev)

    qcols = pl.ds(pl.multiple_of(head * 2 * HEAD, 2 * HEAD), 2 * HEAD)
    kcols = pl.ds(pl.multiple_of(head * HEAD, HEAD), HEAD)

    def dq_step(i, carry):
        s = (slot + i) % 16
        send_out(s, [(dq_st.at[key_rows(ROWS * s), :], dq_out.at[:, qcols], odq_r)], odq_s)
        return carry

    lax.fori_loop(0, 8, dq_step, 0)

    @pl.when(c == 1)
    def _():
        bytes_of(r1.at[1], x1_r.at[1]).wait()
        ship_down(1, tile(3) + r1[1].astype(F32), (0,))

    @pl.when(c == 0)
    def _():
        send_down(1, 1)

    lax.fori_loop(8, 16, dq_step, 0)

    @pl.when(c == 1)
    def _():
        send_down(1, 1)

    ship_core(2, 5 + c)

    @pl.when(c == 0)
    def _():
        bytes_of(r1.at[1], x1_r.at[1]).wait()

    def finish(j, begin, count, extra):
        def span(at):
            return pl.ds(pl.multiple_of(at + begin, 128), count)

        whole = acc[:, span(WINDOW + (2 * j + c) * BLOCK), :]
        whole = whole + r0[j, :, span(0), :].astype(F32)
        if extra is not None:
            whole = whole + extra[:, span(0), :].astype(F32)
        st2[0, span(j * BLOCK), :] = (whole[0] * SCALE).astype(BF)
        st2[1, span(j * BLOCK), :] = whole[1].astype(BF)

        def step(i, carry):
            s = j * 8 + begin // ROWS + i
            send_out(
                s,
                [
                    (st2.at[0, key_rows(ROWS * s), :], dk_out.at[:, kcols], odk_r),
                    (st2.at[1, key_rows(ROWS * s), :], dv_out.at[:, kcols], odv_r),
                ],
                okv_s,
            )
            return carry

        lax.fori_loop(0, count // ROWS, step, 0)

    def await_down(i, h):
        @pl.when(z < PLANES - 1)
        def _():
            bytes_of(r0.at[i, :, half_rows(h), :], x0_r.at[2 * i + h]).wait()

    bytes_of(r1.at[2], x1_r.at[2]).wait()
    await_down(0, 0)
    await_down(0, 1)
    finish(0, 0, BLOCK, r1.at[1 + c])

    @pl.when(c == 0)
    def _():
        acc[:, WINDOW + 2 * BLOCK : WINDOW + 3 * BLOCK, :] += r1[2].astype(F32)

    for h in range(2):
        await_down(1, h)
        finish(1, half_start(h), 128, None)

    bytes_of(kv.at[:, 0:1440, :], snd).wait()

    @pl.when(jnp.logical_not(own))
    def _():
        bytes_of(kv.at[:, 0:96, :], snd0).wait()
        bytes_of(dq_st, odq_s).wait()
        bytes_of(st2, okv_s).wait()

    @pl.when(own)
    def _():
        bytes_of(dq_st.at[0 : HALF - ROWS, :], odq_s).wait()
        bytes_of(st2.at[:, 0 : HALF - ROWS, :], okv_s).wait()

    bytes_of(kv.at[:, 0:HALF, :], snd_o).wait()
    bytes_of(st1, x1_s).wait()

    @pl.when(z < PLANES - 1)
    def _():
        bytes_of(kv.at[:, 0:HALF, :], snd_z).wait()

    @pl.when(z > 0)
    def _():
        bytes_of(kv.at[:, 0:HALF, :], snd_o2).wait()
        bytes_of(st0, x0_s).wait()
    bytes_of(dq_out, odq_r).wait()
    bytes_of(dk_out, odk_r).wait()
    bytes_of(dv_out, odv_r).wait()


def put_kernel(a, b, d, oa, ob, od, sem):
    copies = [
        pltpu.make_async_copy(src, dst, sem.at[i])
        for i, (src, dst) in enumerate(((a, oa), (b, ob), (d, od)))
    ]
    for copy in copies:
        copy.start()
    for copy in copies:
        copy.wait()


def per_device(queries, key_states, value_state_rows, out_grad, doc_lengths):
    any_space = pl.BlockSpec(memory_space=pl.ANY)
    vmem_space = pl.BlockSpec(memory_space=pltpu.VMEM)
    dma = pltpu.SemaphoreType.DMA
    shapes = [queries.shape, key_states.shape, value_state_rows.shape]
    results = pl.pallas_call(
        kernel,
        out_shape=tuple(OUT_SHAPE(s, BF) for s in shapes),
        in_specs=[pl.BlockSpec(memory_space=pltpu.HBM)] * 5,
        out_specs=(OUT_SPEC(),) * 3,
        scratch_shapes=[
            pltpu.VMEM((2, 2 * WINDOW, HEAD), BF),
            pltpu.VMEM((2, 2, HALF, HEAD), BF),
            pltpu.VMEM((1, HALF), jnp.int32),
            pltpu.VMEM((2, 2 * WINDOW, HEAD), F32),
            pltpu.VMEM((HALF, 2 * HEAD), BF),
            pltpu.VMEM((3, 2, BLOCK, HEAD), BF),
            pltpu.VMEM((3, 2, BLOCK, HEAD), BF),
            pltpu.VMEM((2, 2, BLOCK, HEAD), BF),
            pltpu.VMEM((2, 2, BLOCK, HEAD), BF),
            pltpu.VMEM((2, HALF, HEAD), BF),
            pltpu.SMEM((DOCS,), jnp.int32),
            dma, pltpu.SemaphoreType.REGULAR, dma((16,)), dma((16,)), dma, dma((2,)), dma, dma, dma, dma, dma,
            dma, dma((3,)), dma, dma((4,)), dma, dma, dma, dma, dma,
        ],
        compiler_params=pltpu.CompilerParams(
            collective_id=0, has_side_effects=True, vmem_limit_bytes=VLIM * 1024
        ),
        name="window_attention_backward",
    )(queries, key_states, value_state_rows, out_grad, doc_lengths)
    if not PUT:
        return results
    return pl.pallas_call(
        put_kernel,
        out_shape=tuple(jax.ShapeDtypeStruct(s, BF) for s in shapes),
        in_specs=[PUT_SPEC()] * 3,
        out_specs=(any_space,) * 3,
        scratch_shapes=[dma((3,))],
        compiler_params=pltpu.CompilerParams(vmem_limit_bytes=1024 * 1024),
        name="put_results",
    )(*results)


def solution(mesh):
    rows = P(("seq", "tp"), None)
    return jax.shard_map(
        per_device,
        mesh=mesh,
        in_specs=(rows, rows, rows, rows, P()),
        out_specs=(rows, rows, rows),
        check_vma=False,
    )
```
